32 devices in a mesh: freq: 8 (over z, x), panel: 4 (over y, core).
Axes of the slice: x: 2, y: 2, z: 4, core: 2. Of those that a mesh axis runs over, the one named last changes fastest.
Arguments:
- wavefield: float32 [8, 2, 128, 4096], P('freq', None, None, 'panel'), may hold values from -6 to 6
- direct: float32 [8, 2, 128, 4096], P('freq', None, None, 'panel'), may hold values from -6 to 6
- left_factors: float32 [8, 4096, 6, 128], P('freq', 'panel'), may hold values from -0.375 to 0.375
- right_factors: float32 [8, 16, 6, 256, 128], P('freq', 'panel'), may hold values from -0.3125 to 0.3125
- tile_src: int32 [16, 6], P('panel'), may hold values from -1 to 7, as said below
- onset: int32 [128, 2048], P('freq'), may hold values from 128 to 895
Outputs:
- focusing: float32 [8, 2, 128, 4096], P('freq', None, None, 'panel')
The draws below stay inside these ranges and needn't reach their ends.
Inputs may be any that keep to these rules, and one draw needn't show every extreme that they name: `tile_src`: in each receiver panel's row the first k slots name distinct source tiles, with 2 <= k <= 6, and the other slots hold -1; in every aligned block of 4 panels at least one panel fills all 6 slots.
All inputs are finite; a program needn't handle non-finite values.
Results may differ from the reference program's by a relative error of at most 0.0003.
Values sent between devices are 32-bit elements; how exact they have to be, the bound alone decides.
A program may use at most 128 MiB of HBM per device.

```python
import math
import jax
import jax.numpy as jnp
from jax import lax

TILE = 256
RANK = 64
SRC_TILES = 8
SLOTS = 6
VS = 128
NT = 1024
FIRST_BIN = 8
RP_DEV = 4
PANELS = 16
RECV = 4096
SRC = 2048
NF = 8


def draw_tile_src(key, part):
    key_order = jax.random.fold_in(key, 11)
    key_count = jax.random.fold_in(key, 23)
    key_full = jax.random.fold_in(key, 37)
    scores = jax.random.randint(key_order, (PANELS, SRC_TILES), 0, 1 << 20) * SRC_TILES + jnp.arange(SRC_TILES, dtype=jnp.int32)[None, :]
    order = jnp.argsort(scores, axis=1).astype(jnp.int32)[:, :SLOTS]
    counts = jax.random.randint(key_count, (PANELS,), 2, SLOTS + 1)
    full_at = jax.random.randint(key_full, (PANELS // RP_DEV,), 0, RP_DEV)
    position = jnp.arange(PANELS, dtype=jnp.int32) % RP_DEV
    counts = jnp.where(position == jnp.repeat(full_at, RP_DEV), SLOTS, counts)
    slot_index = jnp.arange(SLOTS, dtype=jnp.int32)
    return jnp.where(slot_index[None, :] < counts[:, None], order, -1).astype(jnp.int32)


def set_ends(values, own_key, smallest, top_value):
    extent = values.shape
    index_at = [jax.random.randint(jax.random.fold_in(own_key, axis), (), 0, extent[axis]) for axis in range(len(extent))]
    values = values.at[tuple(index_at)].set(smallest)
    longest = extent.index(max(extent))
    index_at[longest] = (index_at[longest] + 1) % extent[longest]
    return values.at[tuple(index_at)].set(top_value)


def shard_levels(rng, shape, pieces, least, top_value):
    factor_of, own = 1.0, jax.random.fold_in(rng, 6)
    for dim, blocks in pieces:
        draws = jnp.exp(jax.random.uniform(jax.random.fold_in(own, dim), (blocks,), jnp.float32, least / len(pieces), top_value / len(pieces)))
        factor_of = factor_of * jnp.repeat(draws, shape[dim] // blocks).reshape([-1 if axis == dim else 1 for axis in range(len(shape))])
    return factor_of


def centred(own_key, shape, spread, most, pieces=(), kind=jnp.bfloat16):
    drawn = spread * jax.random.normal(own_key, shape, jnp.float32)
    if pieces:
        drawn = drawn * shard_levels(own_key, shape, pieces, -0.22, 0.18)
    return jnp.clip(drawn, -most, most).astype(kind)


def setup_inputs(seed: int = 0) -> dict:
    key_of = jax.random.split(jax.random.key(seed), 7)
    wavefield = centred(key_of[0], (NF, 2, VS, RECV), 1.0, 6.0, ((0, 8), (3, 4)), jnp.float32)
    direct = centred(key_of[1], (NF, 2, VS, RECV), 1.0, 6.0, ((0, 8), (3, 4)), jnp.float32)
    left_factors = centred(key_of[2], (NF, RECV, SLOTS, 2 * RANK), TILE ** -0.5, 0.375, ((0, 8), (1, 4)), jnp.float32)
    right_factors = centred(key_of[3], (NF, PANELS, SLOTS, TILE, 2 * RANK), (RANK * SLOTS) ** -0.5, 0.3125, ((0, 8), (1, 4)), jnp.float32)
    tile_src = draw_tile_src(jax.random.fold_in(key_of[6], 71), 0)
    onset = set_ends(jax.random.randint(key_of[5], (VS, SRC), NT // 8, NT - NT // 8), jax.random.fold_in(key_of[5], 1), NT // 8, (NT - NT // 8) - 1).astype(jnp.int32)
    return {"wavefield": wavefield, "direct": direct, "left_factors": left_factors, "right_factors": right_factors, "tile_src": tile_src, "onset": onset}


HIGH = lax.Precision.HIGHEST

def pair_coef(products):
    half = products.shape[3] // 2
    real_part = products[0, :, :, :half] + products[1, :, :, half:]
    imag_part = products[1, :, :, :half] - products[0, :, :, half:]
    return jnp.stack([jnp.concatenate([real_part, -imag_part], axis=2), jnp.concatenate([imag_part, real_part], axis=2)])

def tile_adjoint(left, right, field, picks):
    products = jnp.einsum('ptsk,cvpt->cpskv', left, field, precision=HIGH)
    contrib = jnp.einsum('pstk,cpskv->cpstv', right, pair_coef(products), precision=HIGH)
    return jnp.einsum('psj,cpstv->cvjt', picks, contrib, precision=HIGH)

def tile_forward(left, right, source_field, picks):
    chosen = jnp.einsum('psj,cvjt->cpsvt', picks, source_field, precision=HIGH)
    products = jnp.einsum('pstk,cpsvt->cpskv', right, chosen, precision=HIGH)
    return jnp.einsum('ptsk,cpskv->cvpt', left, pair_coef(products), precision=HIGH)

def time_tables(count, length):
    times = jnp.arange(length, dtype=jnp.int32)
    freqs = jnp.arange(count, dtype=jnp.int32) + FIRST_BIN
    phase = freqs[None, :] * times[:, None] % length
    angle = 2.0 * math.pi / length * phase.astype(jnp.float32)
    waves = jnp.stack([jnp.cos(angle), -jnp.sin(angle)], axis=2).reshape(length, 2 * count)
    return (waves * (1.0 / math.sqrt(count)), waves.T * (1.0 / math.sqrt(length)))

def gate_block(block, marks, into, outof):
    count = block.shape[0]
    width = block.shape[2]
    length = into.shape[0]
    traces = jnp.dot(into, block.reshape(2 * count, width), precision=HIGH, preferred_element_type=jnp.float32)
    times = jnp.arange(length, dtype=jnp.int32)
    gated = jnp.where(times[:, None] < marks[None, :], traces, jnp.zeros_like(traces))
    back = jnp.dot(outof, gated, precision=HIGH, preferred_element_type=jnp.float32)
    return back.reshape(count, 2, width)

def apply_gate(moved, marks, into, outof):
    items = jnp.moveaxis(moved, 2, 0)
    result = lax.map(lambda pair: gate_block(pair[0], pair[1], into, outof), (items, marks))
    return jnp.moveaxis(result, 0, 2)

def reference(wavefield, direct, left_factors, right_factors, tile_src, onset):
    picks = (tile_src[:, :, None] == jnp.arange(SRC_TILES, dtype=jnp.int32)[None, None, :]).astype(jnp.float32)

    def adjoint_one(args):
        field, left, right = args
        left4 = left.reshape(PANELS, TILE, SLOTS, 2 * RANK)
        field4 = field.reshape(2, VS, PANELS, TILE)
        return tile_adjoint(left4, right, field4, picks).reshape(2, VS, SRC)
    adjoint = lax.map(adjoint_one, (wavefield, left_factors, right_factors))
    into, outof = time_tables(NF, NT)
    back = apply_gate(adjoint, onset, into, outof)

    def forward_one(args):
        source_field, left, right = args
        left4 = left.reshape(PANELS, TILE, SLOTS, 2 * RANK)
        result = tile_forward(left4, right, source_field.reshape(2, VS, SRC_TILES, TILE), picks)
        return result.reshape(2, VS, RECV)
    forward = lax.map(forward_one, (back, left_factors, right_factors))
    return direct - forward
```

```python
import functools
import math

import jax
import jax.numpy as jnp
from jax import lax
from jax.experimental import pallas as pl
from jax.experimental.pallas import tpu as pltpu
from jax.sharding import PartitionSpec as P

NT = 1024
FIRST_BIN = 8
SRC_TILES = 8
LANES = 128
BF16 = jnp.bfloat16
F32 = jnp.float32
NN = (((1,), (0,)), ((), ()))
NT_DIMS = (((1,), (1,)), ((), ()))


def split(x):
    high = x.astype(BF16)
    return high, (x - high.astype(F32)).astype(BF16)


def mxu(a, b, dims):
    return lax.dot_general(a, b, dims, preferred_element_type=F32)


def lanes(*parts):
    return jnp.concatenate(parts, axis=1)


def pair_coef(products):
    rows, width = products.shape
    first, second = products[: rows // 2], products[rows // 2 :]
    lane = lax.broadcasted_iota(jnp.int32, first.shape, 1)
    sign = jnp.where(lane < width // 2, 1.0, -1.0).astype(F32)
    swap = lambda x: pltpu.roll(x, width // 2, 1)
    return jnp.concatenate([first + sign * swap(second), second - sign * swap(first)], axis=0)

def gate_tables(count):
    assert 2 * (FIRST_BIN + count - 1) < NT
    cot = lambda m: 1.0 / math.tan(math.pi * m / NT)
    minus = [[0.0 if f == g else cot(g - f) for g in range(count)] for f in range(count)]
    plus = [[cot(f + g + 2 * FIRST_BIN) for g in range(count)] for f in range(count)]
    real = [[0.5 * (minus[f][g] + plus[f][g]) for g in range(count)] for f in range(count)]
    imag = [[0.5 * (plus[f][g] - minus[f][g]) for g in range(count)] for f in range(count)]
    return real, imag


def gate_map(xr, xi, tables):
    real, imag = tables
    count = len(xr)
    total = functools.reduce(lambda a, b: a + b, xr)
    gr, gi = [], []
    for f in range(count):
        a = 0.5 * xr[f] - total
        b = 0.5 * xi[f]
        for g in range(count):
            a = a + real[f][g] * xi[g]
            b = b + imag[f][g] * xr[g]
        gr.append(a)
        gi.append(b)
    return gr, gi


def gate(xr, xi, c1, s1, mark, tables):
    count = len(xr)
    scale = 0.5 / math.sqrt(count * NT)
    ec, es = c1, s1
    power = 1
    while power * 2 <= FIRST_BIN:
        ec, es = ec * ec - es * es, 2.0 * ec * es
        power *= 2
    while power < FIRST_BIN:
        ec, es = ec * c1 - es * s1, ec * s1 + es * c1
        power += 1
    cs, sn = [], []
    for f in range(count):
        cs.append(ec)
        sn.append(es)
        ec, es = ec * c1 - es * s1, ec * s1 + es * c1
    yr = [xr[f] * cs[f] - xi[f] * sn[f] for f in range(count)]
    yi = [xr[f] * sn[f] + xi[f] * cs[f] for f in range(count)]
    hr, hi = gate_map(yr, yi, tables)
    gr, gi = gate_map(xr, xi, tables)
    br = [scale * (cs[f] * hr[f] + sn[f] * hi[f] - gr[f] + mark * xr[f]) for f in range(count)]
    bi = [scale * (cs[f] * hi[f] - sn[f] * hr[f] - gi[f] + mark * xi[f]) for f in range(count)]
    return br, bi


def unit(mark):
    quarter = NT // 4
    phase = mark & (NT - 1)
    quad = lax.shift_right_logical(phase + quarter // 2, quarter.bit_length() - 1)
    x = (2.0 * math.pi / NT) * (phase - quad * quarter).astype(F32)
    z = x * x
    c = jnp.full_like(x, 1.0 / math.factorial(10))
    s = jnp.full_like(x, 1.0 / math.factorial(11))
    for n in (8, 6, 4, 2, 0):
        c = 1.0 / math.factorial(n) - z * c
    for n in (9, 7, 5, 3, 1):
        s = 1.0 / math.factorial(n) - z * s
    s = s * x
    quad = quad & 3
    swap = (quad & 1) == 1
    cos = jnp.where(swap, s, c)
    sin = jnp.where(swap, c, s)
    cos = jnp.where((quad == 1) | (quad == 2), -cos, cos)
    sin = jnp.where(quad >= 2, -sin, sin)
    return cos, sin


def halves_of(vp):
    return 2 if vp % 16 == 0 else 1


def marchenko_kernel(
    nf, ny, chunks, tile_hbm, onset_hbm, field_hbm, direct_hbm, left_hbm, right_hbm, out_ref,
    tile_ref, onset_ref, field, direct, left, right, fcat, left_h, left_l, right_h, right_l,
    part, buf1, sums, buf2, xbuf, rbuf, obuf, source, chosen_ref,
    tile_sem, onset_sem, field_sem, direct_sem, left_sem, right_sem,
    s1s, s1r, s2s, s2r, s3s, s3r, s4s, s4r, s5s, s5r, s6s, s6r,
):
    tables = gate_tables(nf)
    panels, slots, rows, width = right.shape
    parts, prow = part.shape[3:5]
    pair = parts * prow
    virtual = pair // 2
    vp = virtual // nf
    vh = vp // parts
    aligned = vh % 8 == 0
    blocks = rows // LANES
    np_ = 2 * ny
    tiles = np_ // blocks
    steps = chunks * parts
    me = lax.axis_index("freq")
    q = lax.axis_index("panel")
    y, c = q // 2, q % 2
    partner = {"panel": y * 2 + 1 - c}
    ypeer = [{"panel": ((y + d) % ny) * 2 + c} for d in range(ny)]
    fpeer = [{"freq": (me + d) % nf} for d in range(nf)]
    MESH = pl.DeviceIdType.MESH

    tile_load = pltpu.make_async_copy(tile_hbm, tile_ref, tile_sem)
    onset_load = pltpu.make_async_copy(onset_hbm, onset_ref, onset_sem)
    loads_a, loads_b, loads_c = [], [], []
    for p in range(panels):
        cols = pl.ds(p * rows, rows)
        if aligned:
            group = [
                pltpu.make_async_copy(field_hbm.at[:, :, h, :, cols], field.at[p, h], field_sem.at[p])
                for h in range(parts)
            ]
            for h in range(parts):
                loads_c.append(
                    pltpu.make_async_copy(direct_hbm.at[:, :, h, :, cols], direct.at[p, h], direct_sem)
                )
        else:
            group = [pltpu.make_async_copy(field_hbm.at[:, :, cols], field.at[p], field_sem.at[p])]
            loads_c.append(pltpu.make_async_copy(direct_hbm.at[:, :, cols], direct.at[p], direct_sem))
        group.append(pltpu.make_async_copy(left_hbm.at[:, cols, :], left[p], left_sem.at[p]))
        loads_a.append(group)
        loads_b.append(pltpu.make_async_copy(right_hbm.at[p], right.at[p], right_sem))
    tile_load.start()
    for group in loads_a:
        for copy in group:
            copy.start()
    for copy in loads_b + [onset_load] + loads_c:
        copy.start()

    barrier = pltpu.get_barrier_semaphore()
    for dev in [partner] + ypeer[1:] + fpeer[1:]:
        pl.semaphore_signal(barrier, inc=1, device_id=dev, device_id_type=MESH)

    tile_load.wait()

    def arrived(ref, sem):
        pltpu.make_async_copy(ref, ref, sem).wait()

    def slot_of(p, j):
        slot = jnp.int32(0)
        live = jnp.int32(0)
        for s in range(slots):
            hit = tile_ref[p, s] == j
            slot = jnp.where(hit, jnp.int32(s), slot)
            live = jnp.where(hit, jnp.int32(1), live)
        return slot, live.astype(F32)

    def send(src, dst, ssem, rsem, device):
        copy = pltpu.make_async_remote_copy(
            src_ref=src, dst_ref=dst, send_sem=ssem, recv_sem=rsem, device_id=device, device_id_type=MESH
        )
        copy.start()

    def coef_of(products):
        return jnp.concatenate([pair_coef(products[h * prow : (h + 1) * prow]) for h in range(parts)], axis=0)

    def block(yy, cc, ch):
        return ch * np_ + yy * 2 + cc

    order = list(range(1, ny)) + [0]

    def stage_adjoint(ch):
        first = ch * tiles
        found = [[slot_of(p, first + t) for t in range(tiles)] for p in range(panels)]
        coefs = [[None] * panels for _ in range(tiles)]
        for p in range(panels):
            if ch == 0:
                arrived(field.at[p], field_sem.at[p])
                arrived(left[p], left_sem.at[p])
                fh, fl = split(field[p].reshape(pair, rows))
                fcat[p, :, :rows] = fh
                fcat[p, :, rows : 2 * rows] = fh
                fcat[p, :, 2 * rows :] = fl
            for t0 in range(0, tiles, 2):
                sides = []
                for t in range(t0, min(t0 + 2, tiles)):
                    slot, live = found[p][t]
                    h, l = split(left[p][slot] * live)
                    left_h[p, first + t] = h
                    left_l[p, first + t] = l
                    sides.append(jnp.concatenate([h, l, h], axis=0))
                products = mxu(fcat[p], lanes(*sides), NN)
                for i in range(len(sides)):
                    coefs[t0 + i][p] = split(coef_of(products[:, i * width : (i + 1) * width]))
        for t in range(tiles):
            ins, outs = [], []
            for p in range(panels):
                if ch == 0 and t == 0 and p == 0:
                    arrived(right, right_sem)
                rh, rl = split(right[p, found[p][t][0]])
                right_h[p, first + t] = rh
                right_l[p, first + t] = rl
                h, l = coefs[t][p]
                ins += [h, l, h]
                outs += [rh, rh, rl]
            tile = mxu(lanes(*ins), lanes(*outs), NT_DIMS)
            for b in range(blocks):
                for h in range(parts):
                    part[ch, t, b, h] = tile[h * prow : (h + 1) * prow, b * LANES : (b + 1) * LANES]
        if ch == 0:
            pl.semaphore_wait(barrier, 1 + (ny - 1) + (nf - 1))
        for h in range(parts):
            k = ch * parts + h
            send(part.at[ch, :, 1 - c, h], buf1.at[k], s1s, s1r.at[k], partner)

    def stage_sum(k):
        ch, h = divmod(k, parts)
        arrived(buf1.at[k], s1r.at[k])
        for d in order:
            yy = (y + d) % ny
            sums[k, d] = part[ch, yy, c, h] + buf1[k, yy]
            if d:
                send(sums.at[k, d], buf2.at[k, d - 1], s2s, s2r.at[k], ypeer[d])

    def stage_out(k):
        total = sums[k, 0]
        arrived(buf2.at[k], s2r.at[k])
        for d in range(1, ny):
            total = total + buf2[k, d - 1]
        if aligned:
            xbuf[k] = total.reshape(2, nf, vh, LANES)
        else:
            for i in range(2 * nf):
                xbuf[k, i // nf, i % nf] = total[i * vh : (i + 1) * vh]
        for d in range(1, nf):
            to = (me + d) % nf
            send(xbuf.at[k, :, to], rbuf.at[k, me], s3s, s3r.at[k], fpeer[d])
        rbuf[k, me] = xbuf[k, :, me]

    def stage_gate(k):
        ch, h = divmod(k, parts)
        at = block(y, c, ch)
        if k == 0:
            onset_load.wait()
        mark = onset_ref[h * vh : (h + 1) * vh, pl.ds(pl.multiple_of(at * LANES, LANES), LANES)]
        cos, sin = unit(mark)
        arrived(rbuf.at[k, : nf - 1], s3r.at[k])
        xr = [rbuf[k, f, 0] for f in range(nf)]
        xi = [rbuf[k, f, 1] for f in range(nf)]
        br, bi = gate(xr, xi, cos, sin, mark.astype(F32), tables)
        for f in range(nf):
            obuf[k, f, 0] = br[f]
            obuf[k, f, 1] = bi[f]
        for d in range(1, nf):
            to = (me + d) % nf
            send(obuf.at[k, to], source.at[at, h, :, me], s4s, s4r.at[k], fpeer[d])
        source[at, h, :, me] = obuf[k, me]

    def stage_back(k):
        ch, h = divmod(k, parts)
        arrived(obuf.at[k, : nf - 1], s4r.at[k])
        at = source.at[block(y, c, ch), h]
        for d in range(1, ny):
            send(at, at, s5s, s5r.at[k, d - 1], ypeer[d])
        send(at, at, s6s, s6r.at[ch, 0], partner)

    def stage_pass(k):
        ch, h = divmod(k, parts)
        for d in range(1, ny):
            at = source.at[block((y + ny - d) % ny, c, ch), h]
            arrived(at, s5r.at[k, d - 1])
            send(at, at, s6s, s6r.at[ch, d], partner)

    def load_block(b):
        if aligned:
            return source[b].reshape(pair, LANES)
        for i in range(2 * nf):
            chosen_ref[i * vh : (i + 1) * vh, :] = source[b, 0, i // nf, i % nf]
        return chosen_ref[...]

    seen = []

    def forward(ch, d):
        j = ch * tiles + (y + ny - d) % ny
        arrived(source.at[block((y + ny - d) % ny, 1 - c, ch)], s6r.at[ch, d])
        h, l = split(lanes(*[load_block(j * blocks + b) for b in range(blocks)]))
        rh = lanes(*[right_h[p, j] for p in range(panels)])
        rl = lanes(*[right_l[p, j] for p in range(panels)])
        products = mxu(lanes(h, h, l), jnp.concatenate([rh, rl, rh], axis=0), NN)
        if not seen:
            arrived(direct, direct_sem)
        seen.append((ch, d))
        last = len(seen) == chunks * ny
        for p in range(panels):
            ph, plow = split(coef_of(products[:, p * width : (p + 1) * width]))
            lh, ll = left_h[p, j], left_l[p, j]
            total = mxu(lanes(ph, ph, plow), lanes(lh, ll, lh), NT_DIMS)
            done = direct[p] - total.reshape(direct.shape[1:])
            if not last:
                direct[p] = done
            elif aligned:
                for i in range(parts):
                    out_ref[:, :, i, :, p * rows : (p + 1) * rows] = done[i]
            else:
                out_ref[:, :, p * rows : (p + 1) * rows] = done

    def stage_own(ch):
        forward(ch, 0)

    def stage_forward(ch):
        for d in range(1, ny):
            forward(ch, d)

    assert blocks == 2
    for ch in range(chunks):
        stage_adjoint(ch)
        if ch:
            for h in range(parts):
                stage_sum((ch - 1) * parts + h)
    for h in range(parts):
        stage_sum((chunks - 1) * parts + h)
    for stage, k in schedule(chunks, parts):
        {"out": stage_out, "gate": stage_gate, "back": stage_back, "pass": stage_pass,
         "own": stage_own, "forward": stage_forward}[stage](k)
    arrived(buf1, s1s)
    arrived(buf2, s2s)
    arrived(rbuf.at[:, : nf - 1], s3s)
    arrived(obuf.at[:, : nf - 1], s4s)
    arrived(buf2, s5s)
    arrived(buf1, s6s)


def schedule(chunks, parts):
    steps = chunks * parts
    lags = [("out", 0), ("gate", 4), ("back", 8), ("pass", 10), ("forward", 12), ("own", 9)]
    order = []
    for step in range(2 * steps + 40):
        for stage, lag in lags:
            k = step - lag
            if 0 <= k < steps:
                if stage in ("own", "forward"):
                    if (k + 1) % parts == 0:
                        order.append((stage, k // parts))
                else:
                    order.append((stage, k))
    return order


def shards(nf, npanel, wavefield, direct, left_factors, right_factors, tile_src, onset):
    panels, slots = tile_src.shape
    rows, width = right_factors.shape[3:]
    virtual = wavefield.shape[2]
    blocks = SRC_TILES * rows // LANES
    chunks = blocks // npanel
    ny = npanel // 2
    vp = virtual // nf
    pair = 2 * virtual
    parts = halves_of(vp)
    vh = vp // parts
    steps = chunks * parts
    prow = pair // parts
    left = jnp.transpose(left_factors[0], (1, 0, 2))
    hbm = pl.BlockSpec(memory_space=pl.ANY)
    dma = lambda *n: pltpu.SemaphoreType.DMA(n) if n else pltpu.SemaphoreType.DMA
    split_buf = [pltpu.VMEM((panels, SRC_TILES, rows, width), BF16)] * 2
    if vh % 8 == 0:
        shaped = lambda x: x.reshape(2, nf, parts, vh, x.shape[-1])
        kept = (panels, parts, 2, nf, vh, rows)
    else:
        shaped = lambda x: x
        kept = (panels, 2, virtual, rows)
    field_in, direct_in = shaped(wavefield[0]), shaped(direct[0])
    out = pl.pallas_call(
        functools.partial(marchenko_kernel, nf, ny, chunks),
        in_specs=[hbm] * 6,
        out_specs=pl.BlockSpec(memory_space=pltpu.VMEM),
        out_shape=pltpu.VMEM(direct_in.shape, F32),
        scratch_shapes=[
            pltpu.SMEM(tile_src.shape, jnp.int32),
            pltpu.VMEM(onset.shape, jnp.int32),
            pltpu.VMEM(kept, F32),
            pltpu.VMEM(kept, F32),
            [pltpu.VMEM((slots, rows, width), F32)] * panels,
            pltpu.VMEM((panels, slots, rows, width), F32),
            pltpu.VMEM((panels, pair, 3 * rows), BF16),
            *split_buf,
            *split_buf,
            pltpu.VMEM((chunks, ny, 2, parts, prow, LANES), F32),
            pltpu.VMEM((steps, ny, prow, LANES), F32),
            pltpu.VMEM((steps, ny, prow, LANES), F32),
            pltpu.VMEM((steps, ny - 1, prow, LANES), F32),
            pltpu.VMEM((steps, 2, nf, vh, LANES), F32),
            pltpu.VMEM((steps, nf, 2, vh, LANES), F32),
            pltpu.VMEM((steps, nf, 2, vh, LANES), F32),
            pltpu.VMEM((blocks, parts, 2, nf, vh, LANES), F32),
            pltpu.VMEM((pair, LANES), F32),
            dma(), dma(),
            dma(panels), dma(), dma(panels), dma(),
            dma(), dma(steps), dma(), dma(steps), dma(), dma(steps),
            dma(), dma(steps), dma(), dma(steps, ny - 1), dma(), dma(chunks, ny),
        ],
        compiler_params=pltpu.CompilerParams(collective_id=0, has_side_effects=True),
        name="marchenko",
    )(tile_src, onset, field_in, direct_in, left, right_factors[0])
    return out.reshape(direct.shape)


def solution(mesh):
    in_specs = (
        P("freq", None, None, "panel"),
        P("freq", None, None, "panel"),
        P("freq", "panel", None, None),
        P("freq", "panel", None, None, None),
        P("panel", None),
        P("freq", None),
    )
    out_specs = P("freq", None, None, "panel")
    body = functools.partial(shards, mesh.shape["freq"], mesh.shape["panel"])
    return jax.shard_map(body, mesh=mesh, in_specs=in_specs, out_specs=out_specs, check_vma=False)
```

```python
import functools
import math

import jax
import jax.numpy as jnp
from jax import lax
from jax.experimental import pallas as pl
from jax.experimental.pallas import tpu as pltpu
from jax.sharding import PartitionSpec as P

NT = 1024
FIRST_BIN = 8
SRC_TILES = 8
LANES = 128
BF16 = jnp.bfloat16
F32 = jnp.float32
NN = (((1,), (0,)), ((), ()))
NT_DIMS = (((1,), (1,)), ((), ()))


def split(x):
    high = x.astype(BF16)
    return high, (x - high.astype(F32)).astype(BF16)


def mxu(a, b, dims):
    return lax.dot_general(a, b, dims, preferred_element_type=F32)


def lanes(*parts):
    return jnp.concatenate(parts, axis=1)


def pair_coef(products):
    rows, width = products.shape
    first, second = products[: rows // 2], products[rows // 2 :]
    lane = lax.broadcasted_iota(jnp.int32, first.shape, 1)
    sign = jnp.where(lane < width // 2, 1.0, -1.0).astype(F32)
    swap = lambda x: pltpu.roll(x, width // 2, 1)
    return jnp.concatenate([first + sign * swap(second), second - sign * swap(first)], axis=0)

def gate_tables(count):
    assert 2 * (FIRST_BIN + count - 1) < NT
    cot = lambda m: 1.0 / math.tan(math.pi * m / NT)
    minus = [[0.0 if f == g else cot(g - f) for g in range(count)] for f in range(count)]
    plus = [[cot(f + g + 2 * FIRST_BIN) for g in range(count)] for f in range(count)]
    real = [[0.5 * (minus[f][g] + plus[f][g]) for g in range(count)] for f in range(count)]
    imag = [[0.5 * (plus[f][g] - minus[f][g]) for g in range(count)] for f in range(count)]
    return real, imag


def gate_map(xr, xi, tables):
    real, imag = tables
    count = len(xr)
    total = functools.reduce(lambda a, b: a + b, xr)
    gr, gi = [], []
    for f in range(count):
        a = 0.5 * xr[f] - total
        b = 0.5 * xi[f]
        for g in range(count):
            a = a + real[f][g] * xi[g]
            b = b + imag[f][g] * xr[g]
        gr.append(a)
        gi.append(b)
    return gr, gi


def gate(xr, xi, c1, s1, mark, tables):
    count = len(xr)
    scale = 0.5 / math.sqrt(count * NT)
    ec, es = c1, s1
    power = 1
    while power * 2 <= FIRST_BIN:
        ec, es = ec * ec - es * es, 2.0 * ec * es
        power *= 2
    while power < FIRST_BIN:
        ec, es = ec * c1 - es * s1, ec * s1 + es * c1
        power += 1
    cs, sn = [], []
    for f in range(count):
        cs.append(ec)
        sn.append(es)
        ec, es = ec * c1 - es * s1, ec * s1 + es * c1
    yr = [xr[f] * cs[f] - xi[f] * sn[f] for f in range(count)]
    yi = [xr[f] * sn[f] + xi[f] * cs[f] for f in range(count)]
    hr, hi = gate_map(yr, yi, tables)
    gr, gi = gate_map(xr, xi, tables)
    br = [scale * (cs[f] * hr[f] + sn[f] * hi[f] - gr[f] + mark * xr[f]) for f in range(count)]
    bi = [scale * (cs[f] * hi[f] - sn[f] * hr[f] - gi[f] + mark * xi[f]) for f in range(count)]
    return br, bi


def unit(mark):
    quarter = NT // 4
    phase = mark & (NT - 1)
    quad = lax.shift_right_logical(phase + quarter // 2, quarter.bit_length() - 1)
    x = (2.0 * math.pi / NT) * (phase - quad * quarter).astype(F32)
    z = x * x
    c = jnp.full_like(x, 1.0 / math.factorial(10))
    s = jnp.full_like(x, 1.0 / math.factorial(11))
    for n in (8, 6, 4, 2, 0):
        c = 1.0 / math.factorial(n) - z * c
    for n in (9, 7, 5, 3, 1):
        s = 1.0 / math.factorial(n) - z * s
    s = s * x
    quad = quad & 3
    swap = (quad & 1) == 1
    cos = jnp.where(swap, s, c)
    sin = jnp.where(swap, c, s)
    cos = jnp.where((quad == 1) | (quad == 2), -cos, cos)
    sin = jnp.where(quad >= 2, -sin, sin)
    return cos, sin


def halves_of(vp):
    return 2 if vp % 16 == 0 else 1


def marchenko_kernel(
    nf, ny, chunks, tile_hbm, onset_hbm, field_hbm, direct_hbm, left_hbm, right_hbm, out_ref,
    tile_ref, onset_ref, field, direct, left, right, fcat, left_h, left_l, right_h, right_l,
    part, buf1, sums, buf2, xbuf, rbuf, obuf, source, chosen_ref, xfirst, rfirst, yfirst, ylast,
    tile_sem, onset_sem, field_sem, direct_sem, left_sem, right_sem,
    s1s, s1r, s2s, s2r, s3s, s3r, s4s, s4r, s5s, s5r, s6s, s6r, s7s, s7r, s8s, s8r,
):
    tables = gate_tables(nf)
    panels, slots, rows, width = right.shape
    parts, prow = part.shape[3:5]
    pair = parts * prow
    virtual = pair // 2
    vp = virtual // nf
    vh = vp // parts
    aligned = vh % 8 == 0
    blocks = rows // LANES
    np_ = 2 * ny
    tiles = np_ // blocks
    steps = chunks * parts
    early = late = int(ny == 2)
    me = lax.axis_index("freq")
    q = lax.axis_index("panel")
    y, c = q // 2, q % 2
    partner = {"panel": y * 2 + 1 - c}
    ypeer = [{"panel": ((y + d) % ny) * 2 + c} for d in range(ny)]
    fpeer = [{"freq": (me + d) % nf} for d in range(nf)]
    MESH = pl.DeviceIdType.MESH

    tile_load = pltpu.make_async_copy(tile_hbm, tile_ref, tile_sem)
    onset_load = pltpu.make_async_copy(onset_hbm, onset_ref, onset_sem)
    loads_a, loads_b, loads_c = [], [], []
    for p in range(panels):
        cols = pl.ds(p * rows, rows)
        if aligned:
            group = [
                pltpu.make_async_copy(field_hbm.at[:, :, h, :, cols], field.at[p, h], field_sem.at[p])
                for h in range(parts)
            ]
            for h in range(parts):
                loads_c.append(
                    pltpu.make_async_copy(direct_hbm.at[:, :, h, :, cols], direct.at[p, h], direct_sem)
                )
        else:
            group = [pltpu.make_async_copy(field_hbm.at[:, :, cols], field.at[p], field_sem.at[p])]
            loads_c.append(pltpu.make_async_copy(direct_hbm.at[:, :, cols], direct.at[p], direct_sem))
        group.append(pltpu.make_async_copy(left_hbm.at[:, cols, :], left[p], left_sem.at[p]))
        loads_a.append(group)
        loads_b.append(pltpu.make_async_copy(right_hbm.at[p], right.at[p], right_sem))
    tile_load.start()
    for group in loads_a:
        for copy in group:
            copy.start()

    barrier = pltpu.get_barrier_semaphore()
    for dev in [partner] + ypeer[1:] + fpeer[1:]:
        pl.semaphore_signal(barrier, inc=1, device_id=dev, device_id_type=MESH)

    def arrived(ref, sem):
        pltpu.make_async_copy(ref, ref, sem).wait()

    def slot_of(p, j):
        slot = jnp.int32(0)
        live = jnp.int32(0)
        for s in range(slots):
            hit = tile_ref[p, s] == j
            slot = jnp.where(hit, jnp.int32(s), slot)
            live = jnp.where(hit, jnp.int32(1), live)
        return slot, live.astype(F32)

    def send(src, dst, ssem, rsem, device):
        copy = pltpu.make_async_remote_copy(
            src_ref=src, dst_ref=dst, send_sem=ssem, recv_sem=rsem, device_id=device, device_id_type=MESH
        )
        copy.start()

    def coef_of(products):
        count = products.shape[0] // prow
        return jnp.concatenate([pair_coef(products[h * prow : (h + 1) * prow]) for h in range(count)], axis=0)

    def block(yy, cc, ch):
        return ch * np_ + yy * 2 + cc

    order = list(range(1, ny)) + [0]
    half = prow // 2
    whole = [(slice(0, 2), 0)]

    def lines(i):
        return slice(0, prow) if isinstance(i, slice) else slice(i * half, (i + 1) * half)

    def entering(k):
        return [(0, 0), (1, steps - k)] if k == early else whole

    def leaving(k):
        return [(i, i) for i in range(2)] if k == steps - 1 and not late else whole


    def stage_adjoint(ch):
        first = ch * tiles
        if ch == 0:
            tile_load.wait()
        found = [[slot_of(p, first + t) for t in range(tiles)] for p in range(panels)]
        coefs = [[None] * panels for _ in range(tiles)]
        for p in range(panels):
            if ch == 0:
                arrived(field.at[p], field_sem.at[p])
                arrived(left[p], left_sem.at[p])
                if p == min(1, panels - 1):
                    for copy in loads_b:
                        copy.start()
                fh, fl = split(field[p].reshape(pair, rows))
                fcat[p, :, :rows] = fh
                fcat[p, :, rows : 2 * rows] = fh
                fcat[p, :, 2 * rows :] = fl
            for t0 in range(0, tiles, 2):
                sides = []
                for t in range(t0, min(t0 + 2, tiles)):
                    slot, live = found[p][t]
                    h, l = split(left[p][slot] * live)
                    left_h[p, first + t] = h
                    left_l[p, first + t] = l
                    sides.append(jnp.concatenate([h, l, h], axis=0))
                products = mxu(fcat[p], lanes(*sides), NN)
                for i in range(len(sides)):
                    coefs[t0 + i][p] = split(coef_of(products[:, i * width : (i + 1) * width]))
        for t in range(tiles):
            ins, outs = [], []
            for p in range(panels):
                if ch == 0 and t == 0 and p == 0:
                    arrived(right, right_sem)
                rh, rl = split(right[p, found[p][t][0]])
                right_h[p, first + t] = rh
                right_l[p, first + t] = rl
                h, l = coefs[t][p]
                ins += [h, l, h]
                outs += [rh, rh, rl]
            tile = mxu(lanes(*ins), lanes(*outs), NT_DIMS)
            for b in range(blocks):
                for h in range(parts):
                    part[ch, t, b, h] = tile[h * prow : (h + 1) * prow, b * LANES : (b + 1) * LANES]
        if ch == 0:
            for copy in [onset_load] + loads_c:
                copy.start()
            pl.semaphore_wait(barrier, 1 + (ny - 1) + (nf - 1))
        for h in range(parts):
            k = ch * parts + h
            send(part.at[ch, :, 1 - c, h], buf1.at[k], s1s, s1r.at[k], partner)

    def stage_sum(k):
        ch, h = divmod(k, parts)
        arrived(buf1.at[k], s1r.at[k])
        if k < early:
            for d in range(ny):
                yy = (y + d) % ny
                spread(xfirst.at[d], part[ch, yy, c, h] + buf1[k, yy], 0)
            for d in range(1, nf):
                to = (me + d) % nf
                send(xfirst.at[:, :, to], rfirst.at[:, me], s7s, s7r, fpeer[d])
            rfirst[:, me] = xfirst[:, :, me]
            return
        for d in order:
            yy = (y + d) % ny
            sums[k, d] = part[ch, yy, c, h] + buf1[k, yy]
            if d:
                for i, at in entering(k):
                    send(sums.at[k, d, lines(i)], buf2.at[k, d - 1, lines(i)], s2s, s2r.at[k + at], ypeer[d])

    def spread(ref, total, first):
        for r in range(total.shape[0] // vh):
            ref[first + r // nf, r % nf] = total[r * vh : (r + 1) * vh]

    def stage_out(k):
        if k < early:
            arrived(rfirst.at[:, : nf - 1], s7r)
            for d in range(1, ny):
                send(rfirst.at[d], yfirst.at[d - 1], s2s, s2r.at[k], ypeer[d])
            return
        for i, at in entering(k):
            total = sums[k, 0, lines(i)]
            arrived(buf2.at[k, :, lines(i)], s2r.at[k + at])
            for d in range(1, ny):
                total = total + buf2[k, d - 1, lines(i)]
            spread(xbuf.at[k], total, 0 if isinstance(i, slice) else i)
            for d in range(1, nf):
                to = (me + d) % nf
                send(xbuf.at[k, i, to], rbuf.at[k, me, i], s3s, s3r.at[k], fpeer[d])
        rbuf[k, me] = xbuf[k, :, me]

    def stage_gate(k):
        ch, h = divmod(k, parts)
        at = block(y, c, ch)
        if not gates:
            onset_load.wait()
        gates.append(k)
        mark = onset_ref[h * vh : (h + 1) * vh, pl.ds(pl.multiple_of(at * LANES, LANES), LANES)]
        cos, sin = unit(mark)
        if k < early:
            arrived(yfirst, s2r.at[k])
            both = [[rfirst[0, f, i] for f in range(nf)] for i in range(2)]
            for d in range(1, ny):
                both = [[both[i][f] + yfirst[d - 1, f, i] for f in range(nf)] for i in range(2)]
            xr, xi = both
        else:
            arrived(rbuf.at[k, : nf - 1], s3r.at[k])
            xr = [rbuf[k, f, 0] for f in range(nf)]
            xi = [rbuf[k, f, 1] for f in range(nf)]
        br, bi = gate(xr, xi, cos, sin, mark.astype(F32), tables)
        for f in range(nf):
            obuf[k, f, 0] = br[f]
            obuf[k, f, 1] = bi[f]
        for i, sem in leaving(k):
            for d in range(1, nf):
                to = (me + d) % nf
                send(obuf.at[k, to, i], source.at[at, h, i, me], s4s, s4r.at[k + sem], fpeer[d])
        source[at, h, :, me] = obuf[k, me]
        if k >= steps - late:
            for d in range(1, ny):
                send(obuf.at[k], ylast.at[d - 1], s5s, s5r.at[k, d - 1], ypeer[d])

    def stage_cross(k):
        ch, h = divmod(k, parts)
        for d in range(1, ny):
            arrived(ylast.at[d - 1], s5r.at[k, d - 1])
            there = block((y + ny - d) % ny, c, ch)
            for e in range(1, nf):
                to = (me + e) % nf
                send(ylast.at[d - 1, to], source.at[there, h, :, me], s8s, s8r.at[d - 1], fpeer[e])
            source[there, h, :, me] = ylast[d - 1, me]

    def stage_back(k):
        ch, h = divmod(k, parts)
        for i, sem in leaving(k):
            arrived(obuf.at[k, : nf - 1, i], s4r.at[k + sem])
            at = source.at[block(y, c, ch), h, i]
            if k < steps - late:
                for d in range(1, ny):
                    send(at, at, s5s, s5r.at[k + sem, d - 1], ypeer[d])
            send(at, at, s6s, s6r.at[lot(k), 0], partner)

    def stage_pass(k):
        ch, h = divmod(k, parts)
        for i, sem in leaving(k):
            for d in range(1, ny):
                at = source.at[block((y + ny - d) % ny, c, ch), h, i]
                if k < steps - late:
                    arrived(at, s5r.at[k + sem, d - 1])
                else:
                    arrived(obuf.at[k, : nf - 1], s8r.at[d - 1])
                send(at, at, s6s, s6r.at[lot(k), d], partner)

    def lot(k):
        return k // parts if k < (chunks - 1) * parts else chunks - 1 + k % parts

    def load_block(b, hs):
        if aligned:
            return source[b, hs[0] : hs[-1] + 1].reshape(len(hs) * prow, LANES)
        for i in range(2 * nf):
            chosen_ref[i * vh : (i + 1) * vh, :] = source[b, 0, i // nf, i % nf]
        return chosen_ref[...]

    seen = [0] * parts
    gates = []

    def forward(ch, d, hs):
        j = ch * tiles + (y + ny - d) % ny
        there = block((y + ny - d) % ny, 1 - c, ch)
        if ch < chunks - 1:
            arrived(source.at[there], s6r.at[ch, d])
        else:
            for i in hs:
                arrived(source.at[there, i], s6r.at[ch + i, d])
        h, l = split(lanes(*[load_block(j * blocks + b, hs) for b in range(blocks)]))
        rh = lanes(*[right_h[p, j] for p in range(panels)])
        rl = lanes(*[right_l[p, j] for p in range(panels)])
        products = mxu(lanes(h, h, l), jnp.concatenate([rh, rl, rh], axis=0), NN)
        if not any(seen):
            arrived(direct, direct_sem)
        for i in hs:
            seen[i] += 1
        for p in range(panels):
            ph, plow = split(coef_of(products[:, p * width : (p + 1) * width]))
            lh, ll = left_h[p, j], left_l[p, j]
            total = mxu(lanes(ph, ph, plow), lanes(lh, ll, lh), NT_DIMS)
            for n, i in enumerate(hs):
                mine = total[n * prow : (n + 1) * prow]
                if not aligned:
                    done = direct[p] - mine.reshape(direct.shape[1:])
                    if seen[i] == chunks * ny:
                        out_ref[:, :, p * rows : (p + 1) * rows] = done
                    else:
                        direct[p] = done
                else:
                    done = direct[p, i] - mine.reshape(direct.shape[2:])
                    if seen[i] == chunks * ny:
                        out_ref[:, :, i, :, p * rows : (p + 1) * rows] = done
                    else:
                        direct[p, i] = done

    def stage_own(k):
        forward(k // parts, 0, list(range(parts)))

    def stage_forward(k):
        for d in range(1, ny):
            forward(k // parts, d, list(range(parts)))

    def stage_near(k):
        forward(k // parts, 0, [k % parts])

    def stage_far(k):
        for d in range(1, ny):
            forward(k // parts, d, [k % parts])

    assert blocks == 2
    run = {"adjoint": stage_adjoint, "sum": stage_sum, "out": stage_out, "gate": stage_gate, "back": stage_back,
           "pass": stage_pass, "cross": stage_cross, "own": stage_own, "forward": stage_forward, "near": stage_near, "far": stage_far}
    for stage, k in schedule(chunks, parts, late):
        run[stage](k)
    arrived(buf1, s1s)
    arrived(buf2, s2s)
    arrived(rbuf.at[early:, : nf - 1], s3s)
    if early:
        arrived(rfirst.at[:, : nf - 1], s7s)
    arrived(obuf.at[:, : nf - 1], s4s)
    arrived(buf2, s5s)
    if late:
        arrived(ylast.at[:, : nf - 1], s8s)
    arrived(buf1, s6s)


LAGS = {
    "adjoint": -8, "sum": -5.5, "out": 0, "gate": 2.5, "cross": 5.2, "back": 5.3, "pass": 6.3, "own": 6.4, "forward": 7.4,
}
ORDER = [
    ("adjoint", 0), ("adjoint", 1), ("sum", 0), ("sum", 1), ("sum", 2), ("adjoint", 2), ("sum", 3), ("sum", 4),
    ("sum", 5), ("out", 1), ("out", 2), ("out", 3), ("out", 0), ("adjoint", 3), ("out", 4), ("sum", 6), ("gate", 1),
    ("sum", 7), ("out", 5), ("gate", 0), ("out", 6), ("gate", 3), ("out", 7), ("back", 1), ("gate", 2), ("gate", 5),
    ("gate", 4), ("pass", 1), ("back", 0), ("back", 3), ("own", 1), ("gate", 6), ("gate", 7), ("back", 2),
    ("back", 5), ("own", 3), ("cross", 7), ("pass", 3), ("back", 4), ("pass", 0), ("back", 6), ("pass", 2),
    ("own", 5), ("forward", 1), ("back", 7), ("pass", 5), ("forward", 3), ("pass", 4), ("own", 7), ("pass", 7),
    ("pass", 6), ("forward", 5), ("forward", 7),
]


def schedule(chunks, parts, late):
    steps = chunks * parts
    names = ["sum", "out", "gate", "back", "pass"]
    ops = [("adjoint", ch) for ch in range(chunks)]
    for k in range(steps):
        ops += [(name, k) for name in names]
        if k >= steps - late:
            ops.append(("cross", k))
        if k % parts == parts - 1:
            ops += [("own", k), ("forward", k)]
    if late and len(ops) == len(ORDER):
        assert sorted(ops) == sorted(ORDER)
        return ORDER
    place = lambda op: LAGS[op[0]] + op[1] * (parts if op[0] == "adjoint" else 1)
    return sorted(ops, key=place)


def shards(nf, npanel, wavefield, direct, left_factors, right_factors, tile_src, onset):
    panels, slots = tile_src.shape
    rows, width = right_factors.shape[3:]
    virtual = wavefield.shape[2]
    blocks = SRC_TILES * rows // LANES
    chunks = blocks // npanel
    ny = npanel // 2
    vp = virtual // nf
    pair = 2 * virtual
    parts = halves_of(vp)
    vh = vp // parts
    steps = chunks * parts
    prow = pair // parts
    left = jnp.transpose(left_factors[0], (1, 0, 2))
    hbm = pl.BlockSpec(memory_space=pl.ANY)
    dma = lambda *n: pltpu.SemaphoreType.DMA(n) if n else pltpu.SemaphoreType.DMA
    split_buf = [pltpu.VMEM((panels, SRC_TILES, rows, width), BF16)] * 2
    if vh % 8 == 0:
        shaped = lambda x: x.reshape(2, nf, parts, vh, x.shape[-1])
        kept = (panels, parts, 2, nf, vh, rows)
    else:
        shaped = lambda x: x
        kept = (panels, 2, virtual, rows)
    field_in, direct_in = shaped(wavefield[0]), shaped(direct[0])
    out = pl.pallas_call(
        functools.partial(marchenko_kernel, nf, ny, chunks),
        in_specs=[hbm] * 6,
        out_specs=pl.BlockSpec(memory_space=pltpu.VMEM),
        out_shape=pltpu.VMEM(direct_in.shape, F32),
        scratch_shapes=[
            pltpu.SMEM(tile_src.shape, jnp.int32),
            pltpu.VMEM(onset.shape, jnp.int32),
            pltpu.VMEM(kept, F32),
            pltpu.VMEM(kept, F32),
            [pltpu.VMEM((slots, rows, width), F32)] * panels,
            pltpu.VMEM((panels, slots, rows, width), F32),
            pltpu.VMEM((panels, pair, 3 * rows), BF16),
            *split_buf,
            *split_buf,
            pltpu.VMEM((chunks, ny, 2, parts, prow, LANES), F32),
            pltpu.VMEM((steps, ny, prow, LANES), F32),
            pltpu.VMEM((steps, ny, prow, LANES), F32),
            pltpu.VMEM((steps, ny - 1, prow, LANES), F32),
            pltpu.VMEM((steps, 2, nf, vh, LANES), F32),
            pltpu.VMEM((steps, nf, 2, vh, LANES), F32),
            pltpu.VMEM((steps, nf, 2, vh, LANES), F32),
            pltpu.VMEM((blocks, parts, 2, nf, vh, LANES), F32),
            pltpu.VMEM((pair, LANES), F32),
            pltpu.VMEM((ny, 2, nf, vh, LANES), F32),
            pltpu.VMEM((ny, nf, 2, vh, LANES), F32),
            pltpu.VMEM((ny - 1, nf, 2, vh, LANES), F32),
            pltpu.VMEM((ny - 1, nf, 2, vh, LANES), F32),
            dma(), dma(),
            dma(panels), dma(), dma(panels), dma(),
            dma(), dma(steps), dma(), dma(steps + 1), dma(), dma(steps),
            dma(), dma(steps + 1), dma(), dma(steps + 1, ny - 1), dma(), dma(chunks - 1 + parts, ny),
            dma(), dma(), dma(), dma(ny - 1),
        ],
        compiler_params=pltpu.CompilerParams(collective_id=0, has_side_effects=True),
        name="marchenko",
    )(tile_src, onset, field_in, direct_in, left, right_factors[0])
    return out.reshape(direct.shape)


def solution(mesh):
    in_specs = (
        P("freq", None, None, "panel"),
        P("freq", None, None, "panel"),
        P("freq", "panel", None, None),
        P("freq", "panel", None, None, None),
        P("panel", None),
        P("freq", None),
    )
    out_specs = P("freq", None, None, "panel")
    body = functools.partial(shards, mesh.shape["freq"], mesh.shape["panel"])
    return jax.shard_map(body, mesh=mesh, in_specs=in_specs, out_specs=out_specs, check_vma=False)
```

```python
import functools
import math

import jax
import jax.numpy as jnp
from jax import lax
from jax.experimental import pallas as pl
from jax.experimental.pallas import tpu as pltpu
from jax.sharding import PartitionSpec as P

NT = 1024
FIRST_BIN = 8
SRC_TILES = 8
LANES = 128
BF16 = jnp.bfloat16
F32 = jnp.float32
NN = (((1,), (0,)), ((), ()))
NT_DIMS = (((1,), (1,)), ((), ()))


def split(x):
    high = x.astype(BF16)
    return high, (x - high.astype(F32)).astype(BF16)


def mxu(a, b, dims):
    return lax.dot_general(a, b, dims, preferred_element_type=F32)


def lanes(*parts):
    return jnp.concatenate(parts, axis=1)


def pair_coef(products):
    rows, width = products.shape
    first, second = products[: rows // 2], products[rows // 2 :]
    lane = lax.broadcasted_iota(jnp.int32, first.shape, 1)
    sign = jnp.where(lane < width // 2, 1.0, -1.0).astype(F32)
    swap = lambda x: pltpu.roll(x, width // 2, 1)
    return jnp.concatenate([first + sign * swap(second), second - sign * swap(first)], axis=0)

def gate_tables(count):
    assert 2 * (FIRST_BIN + count - 1) < NT
    cot = lambda m: 1.0 / math.tan(math.pi * m / NT)
    minus = [[0.0 if f == g else cot(g - f) for g in range(count)] for f in range(count)]
    plus = [[cot(f + g + 2 * FIRST_BIN) for g in range(count)] for f in range(count)]
    real = [[0.5 * (minus[f][g] + plus[f][g]) for g in range(count)] for f in range(count)]
    imag = [[0.5 * (plus[f][g] - minus[f][g]) for g in range(count)] for f in range(count)]
    return real, imag


def gate_map(xr, xi, tables):
    real, imag = tables
    count = len(xr)
    total = functools.reduce(lambda a, b: a + b, xr)
    gr, gi = [], []
    for f in range(count):
        a = 0.5 * xr[f] - total
        b = 0.5 * xi[f]
        for g in range(count):
            a = a + real[f][g] * xi[g]
            b = b + imag[f][g] * xr[g]
        gr.append(a)
        gi.append(b)
    return gr, gi


def gate(xr, xi, c1, s1, mark, tables):
    count = len(xr)
    scale = 0.5 / math.sqrt(count * NT)
    ec, es = c1, s1
    power = 1
    while power * 2 <= FIRST_BIN:
        ec, es = ec * ec - es * es, 2.0 * ec * es
        power *= 2
    while power < FIRST_BIN:
        ec, es = ec * c1 - es * s1, ec * s1 + es * c1
        power += 1
    cs, sn = [], []
    for f in range(count):
        cs.append(ec)
        sn.append(es)
        ec, es = ec * c1 - es * s1, ec * s1 + es * c1
    yr = [xr[f] * cs[f] - xi[f] * sn[f] for f in range(count)]
    yi = [xr[f] * sn[f] + xi[f] * cs[f] for f in range(count)]
    hr, hi = gate_map(yr, yi, tables)
    gr, gi = gate_map(xr, xi, tables)
    br = [scale * (cs[f] * hr[f] + sn[f] * hi[f] - gr[f] + mark * xr[f]) for f in range(count)]
    bi = [scale * (cs[f] * hi[f] - sn[f] * hr[f] - gi[f] + mark * xi[f]) for f in range(count)]
    return br, bi


def unit(mark):
    quarter = NT // 4
    phase = mark & (NT - 1)
    quad = lax.shift_right_logical(phase + quarter // 2, quarter.bit_length() - 1)
    x = (2.0 * math.pi / NT) * (phase - quad * quarter).astype(F32)
    z = x * x
    c = jnp.full_like(x, 1.0 / math.factorial(10))
    s = jnp.full_like(x, 1.0 / math.factorial(11))
    for n in (8, 6, 4, 2, 0):
        c = 1.0 / math.factorial(n) - z * c
    for n in (9, 7, 5, 3, 1):
        s = 1.0 / math.factorial(n) - z * s
    s = s * x
    quad = quad & 3
    swap = (quad & 1) == 1
    cos = jnp.where(swap, s, c)
    sin = jnp.where(swap, c, s)
    cos = jnp.where((quad == 1) | (quad == 2), -cos, cos)
    sin = jnp.where(quad >= 2, -sin, sin)
    return cos, sin


def halves_of(vp):
    return 2 if vp % 16 == 0 else 1


def marchenko_kernel(
    nf, ny, chunks, early, late, tile_hbm, onset_hbm, field_hbm, direct_hbm, left_hbm, right_hbm, out_ref,
    tile_ref, onset_ref, field, direct, left, right, fcat, left_h, left_l, right_h, right_l,
    part, buf1, sums, buf2, xbuf, rbuf, obuf, source, chosen_ref, xfirst, rfirst, yfirst, ylast,
    tile_sem, onset_sem, field_sem, direct_sem, left_sem, right_sem,
    s1s, s1r, s2s, s2r, s3s, s3r, s4s, s4r, s5s, s5r, s6s, s6r, s7s, s7r, s8s, s8r,
):
    tables = gate_tables(nf)
    panels, (slots, rows, width) = len(right), right[0].shape
    parts, prow = part.shape[3:5]
    pair = parts * prow
    virtual = pair // 2
    vp = virtual // nf
    vh = vp // parts
    aligned = vh % 8 == 0
    blocks = rows // LANES
    np_ = 2 * ny
    tiles = np_ // blocks
    steps = chunks * parts
    me = lax.axis_index("freq")
    q = lax.axis_index("panel")
    y, c = q // 2, q % 2
    partner = {"panel": y * 2 + 1 - c}
    ypeer = [{"panel": ((y + d) % ny) * 2 + c} for d in range(ny)]
    fpeer = [{"freq": (me + d) % nf} for d in range(nf)]
    MESH = pl.DeviceIdType.MESH

    tile_load = pltpu.make_async_copy(tile_hbm, tile_ref, tile_sem)
    onset_load = pltpu.make_async_copy(onset_hbm, onset_ref, onset_sem)
    loads_a, loads_b, loads_c = [], [], []
    for p in range(panels):
        cols = pl.ds(p * rows, rows)
        if aligned:
            group = [
                pltpu.make_async_copy(field_hbm.at[:, :, h, :, cols], field.at[p, h], field_sem)
                for h in range(parts)
            ]
            for h in range(parts):
                loads_c.append(
                    pltpu.make_async_copy(direct_hbm.at[:, :, h, :, cols], direct.at[p, h], direct_sem)
                )
        else:
            group = [pltpu.make_async_copy(field_hbm.at[:, :, cols], field.at[p], field_sem)]
            loads_c.append(pltpu.make_async_copy(direct_hbm.at[:, :, cols], direct.at[p], direct_sem))
        group.append(pltpu.make_async_copy(left_hbm.at[:, cols, :], left[p], left_sem.at[p]))
        loads_a.append(group)
        loads_b.append(pltpu.make_async_copy(right_hbm.at[p], right[p], right_sem.at[p]))
    tile_load.start()
    for group in loads_a:
        for copy in group[:-1]:
            copy.start()
    for group in loads_a:
        group[-1].start()

    barrier = pltpu.get_barrier_semaphore()
    for dev in [partner] + ypeer[1:] + fpeer[1:]:
        pl.semaphore_signal(barrier, inc=1, device_id=dev, device_id_type=MESH)

    def arrived(ref, sem):
        pltpu.make_async_copy(ref, ref, sem).wait()

    def slot_of(p, j):
        slot = jnp.int32(0)
        live = jnp.int32(0)
        for s in range(slots):
            hit = tile_ref[p, s] == j
            slot = jnp.where(hit, jnp.int32(s), slot)
            live = jnp.where(hit, jnp.int32(1), live)
        return slot, live.astype(F32)

    def send(src, dst, ssem, rsem, device):
        copy = pltpu.make_async_remote_copy(
            src_ref=src, dst_ref=dst, send_sem=ssem, recv_sem=rsem, device_id=device, device_id_type=MESH
        )
        copy.start()

    def coef_of(products):
        count = products.shape[0] // prow
        return jnp.concatenate([pair_coef(products[h * prow : (h + 1) * prow]) for h in range(count)], axis=0)

    def block(yy, cc, ch):
        return ch * np_ + yy * 2 + cc

    order = list(range(1, ny)) + [0]
    half = prow // 2
    whole = [(slice(0, 2), 0)]

    def lines(i):
        return slice(0, prow) if isinstance(i, slice) else slice(i * half, (i + 1) * half)

    def entering(k):
        return [(0, 0), (1, steps - k)] if k == early else whole

    def leaving(k):
        return [(i, i) for i in range(2)] if k == steps - 1 and not late else whole


    def stage_adjoint(ch):
        first = ch * tiles
        if ch == 0:
            tile_load.wait()
            for copy in loads_b:
                copy.start()
            arrived(field, field_sem)
            for p in range(panels):
                fh, fl = split(field[p].reshape(pair, rows))
                fcat[p, :, :rows] = fh
                fcat[p, :, rows : 2 * rows] = fh
                fcat[p, :, 2 * rows :] = fl
            for p in range(panels):
                arrived(left[p], left_sem.at[p])
        found = [[slot_of(p, first + t) for t in range(tiles)] for p in range(panels)]
        coefs = [[None] * panels for _ in range(tiles)]
        for p in range(panels):
            for t0 in range(0, tiles, 2):
                sides = []
                for t in range(t0, min(t0 + 2, tiles)):
                    slot, live = found[p][t]
                    h, l = split(left[p][slot] * live)
                    left_h[p, first + t] = h
                    left_l[p, first + t] = l
                    sides.append(jnp.concatenate([h, l, h], axis=0))
                products = mxu(fcat[p], lanes(*sides), NN)
                for i in range(len(sides)):
                    coefs[t0 + i][p] = split(coef_of(products[:, i * width : (i + 1) * width]))
        step = (panels + 1) // 2 if ch == 0 else panels
        sums_t = [None] * tiles
        for p0 in range(0, panels, step):
            for t in range(tiles):
                ins, outs = [], []
                for p in range(p0, min(p0 + step, panels)):
                    if ch == 0 and t == 0:
                        arrived(right[p], right_sem.at[p])
                    rh, rl = split(right[p][found[p][t][0]])
                    right_h[p, first + t] = rh
                    right_l[p, first + t] = rl
                    h, l = coefs[t][p]
                    ins += [h, l, h]
                    outs += [rh, rh, rl]
                more = mxu(lanes(*ins), lanes(*outs), NT_DIMS)
                sums_t[t] = more if p0 == 0 else sums_t[t] + more
        for t, tile in enumerate(sums_t):
            for b in range(blocks):
                for h in range(parts):
                    part[ch, t, b, h] = tile[h * prow : (h + 1) * prow, b * LANES : (b + 1) * LANES]
        if ch == 0:
            for copy in [onset_load] + loads_c:
                copy.start()
            pl.semaphore_wait(barrier, 1 + (ny - 1) + (nf - 1))
        for h in range(parts):
            k = ch * parts + h
            send(part.at[ch, :, 1 - c, h], buf1.at[k], s1s, s1r.at[k], partner)

    def stage_sum(k):
        ch, h = divmod(k, parts)
        arrived(buf1.at[k], s1r.at[k])
        if k < early:
            for d in range(ny):
                yy = (y + d) % ny
                spread(xfirst.at[k, d], part[ch, yy, c, h] + buf1[k, yy], 0)
            for d in range(1, nf):
                to = (me + d) % nf
                send(xfirst.at[k, :, :, to], rfirst.at[k, :, me], s7s, s7r.at[k], fpeer[d])
            rfirst[k, :, me] = xfirst[k, :, :, me]
            return
        for d in order:
            yy = (y + d) % ny
            sums[k, d] = part[ch, yy, c, h] + buf1[k, yy]
            if d:
                for i, at in entering(k):
                    send(sums.at[k, d, lines(i)], buf2.at[k, d - 1, lines(i)], s2s, s2r.at[k + at], ypeer[d])

    def spread(ref, total, first):
        for r in range(total.shape[0] // vh):
            ref[first + r // nf, r % nf] = total[r * vh : (r + 1) * vh]

    def stage_out(k):
        if k < early:
            arrived(rfirst.at[k, :, : nf - 1], s7r.at[k])
            for d in range(1, ny):
                send(rfirst.at[k, d], yfirst.at[k, d - 1], s2s, s2r.at[k], ypeer[d])
            return
        for i, at in entering(k):
            total = sums[k, 0, lines(i)]
            arrived(buf2.at[k, :, lines(i)], s2r.at[k + at])
            for d in range(1, ny):
                total = total + buf2[k, d - 1, lines(i)]
            spread(xbuf.at[k], total, 0 if isinstance(i, slice) else i)
            for d in range(1, nf):
                to = (me + d) % nf
                send(xbuf.at[k, i, to], rbuf.at[k, me, i], s3s, s3r.at[k], fpeer[d])
        rbuf[k, me] = xbuf[k, :, me]

    def stage_gate(k):
        ch, h = divmod(k, parts)
        at = block(y, c, ch)
        if not gates:
            onset_load.wait()
        gates.append(k)
        mark = onset_ref[h * vh : (h + 1) * vh, pl.ds(pl.multiple_of(at * LANES, LANES), LANES)]
        cos, sin = unit(mark)
        if k < early:
            arrived(yfirst.at[k], s2r.at[k])
            both = [[rfirst[k, 0, f, i] for f in range(nf)] for i in range(2)]
            for d in range(1, ny):
                both = [[both[i][f] + yfirst[k, d - 1, f, i] for f in range(nf)] for i in range(2)]
            xr, xi = both
        else:
            arrived(rbuf.at[k, : nf - 1], s3r.at[k])
            xr = [rbuf[k, f, 0] for f in range(nf)]
            xi = [rbuf[k, f, 1] for f in range(nf)]
        br, bi = gate(xr, xi, cos, sin, mark.astype(F32), tables)
        for f in range(nf):
            obuf[k, f, 0] = br[f]
            obuf[k, f, 1] = bi[f]
        for i, sem in leaving(k):
            for d in range(1, nf):
                to = (me + d) % nf
                send(obuf.at[k, to, i], source.at[at, h, i, me], s4s, s4r.at[k + sem], fpeer[d])
        source[at, h, :, me] = obuf[k, me]
        if k >= steps - late:
            for d in range(1, ny):
                send(obuf.at[k], ylast.at[d - 1], s5s, s5r.at[k, d - 1], ypeer[d])

    def stage_cross(k):
        ch, h = divmod(k, parts)
        for d in range(1, ny):
            arrived(ylast.at[d - 1], s5r.at[k, d - 1])
            there = block((y + ny - d) % ny, c, ch)
            for e in range(1, nf):
                to = (me + e) % nf
                send(ylast.at[d - 1, to], source.at[there, h, :, me], s8s, s8r.at[d - 1], fpeer[e])
            source[there, h, :, me] = ylast[d - 1, me]

    def stage_back(k):
        ch, h = divmod(k, parts)
        for i, sem in leaving(k):
            arrived(obuf.at[k, : nf - 1, i], s4r.at[k + sem])
            at = source.at[block(y, c, ch), h, i]
            if k < steps - late:
                for d in range(1, ny):
                    send(at, at, s5s, s5r.at[k + sem, d - 1], ypeer[d])
            send(at, at, s6s, s6r.at[ch, 0], partner)

    def stage_pass(k):
        ch, h = divmod(k, parts)
        for i, sem in leaving(k):
            for d in range(1, ny):
                at = source.at[block((y + ny - d) % ny, c, ch), h, i]
                if k < steps - late:
                    arrived(at, s5r.at[k + sem, d - 1])
                else:
                    arrived(obuf.at[k, : nf - 1], s8r.at[d - 1])
                send(at, at, s6s, s6r.at[ch, d], partner)

    def load_block(b, hs):
        if aligned:
            return source[b, hs[0] : hs[-1] + 1].reshape(len(hs) * prow, LANES)
        for i in range(2 * nf):
            chosen_ref[i * vh : (i + 1) * vh, :] = source[b, 0, i // nf, i % nf]
        return chosen_ref[...]

    seen = [0] * parts
    gates = []

    def forward(ch, d, hs):
        j = ch * tiles + (y + ny - d) % ny
        there = block((y + ny - d) % ny, 1 - c, ch)
        arrived(source.at[there], s6r.at[ch, d])
        h, l = split(lanes(*[load_block(j * blocks + b, hs) for b in range(blocks)]))
        rh = lanes(*[right_h[p, j] for p in range(panels)])
        rl = lanes(*[right_l[p, j] for p in range(panels)])
        products = mxu(lanes(h, h, l), jnp.concatenate([rh, rl, rh], axis=0), NN)
        if not any(seen):
            arrived(direct, direct_sem)
        for i in hs:
            seen[i] += 1
        for p in range(panels):
            ph, plow = split(coef_of(products[:, p * width : (p + 1) * width]))
            lh, ll = left_h[p, j], left_l[p, j]
            total = mxu(lanes(ph, ph, plow), lanes(lh, ll, lh), NT_DIMS)
            for n, i in enumerate(hs):
                mine = total[n * prow : (n + 1) * prow]
                if not aligned:
                    done = direct[p] - mine.reshape(direct.shape[1:])
                    if seen[i] == chunks * ny:
                        out_ref[:, :, p * rows : (p + 1) * rows] = done
                    else:
                        direct[p] = done
                else:
                    done = direct[p, i] - mine.reshape(direct.shape[2:])
                    if seen[i] == chunks * ny:
                        out_ref[:, :, i, :, p * rows : (p + 1) * rows] = done
                    else:
                        direct[p, i] = done

    def stage_own(k):
        forward(k // parts, 0, list(range(parts)))

    def stage_forward(k):
        for d in range(1, ny):
            forward(k // parts, d, list(range(parts)))

    assert blocks == 2
    run = {"adjoint": stage_adjoint, "sum": stage_sum, "out": stage_out, "gate": stage_gate, "back": stage_back,
           "pass": stage_pass, "cross": stage_cross, "own": stage_own, "forward": stage_forward}
    for stage, k in schedule(chunks, parts, late):
        run[stage](k)
    arrived(buf1, s1s)
    arrived(buf2, s2s)
    arrived(rbuf.at[early:, : nf - 1], s3s)
    if early:
        arrived(rfirst.at[:, :, : nf - 1], s7s)
    arrived(obuf.at[:, : nf - 1], s4s)
    arrived(buf2, s5s)
    if late:
        arrived(ylast.at[:, : nf - 1], s8s)
    arrived(buf1, s6s)


LAGS = {
    "adjoint": -8, "sum": -5.5, "out": 0, "gate": 2.5, "cross": 5.2, "back": 5.3, "pass": 6.3, "own": 6.4, "forward": 7.4,
}
ORDER = [
    ("adjoint", 0), ("adjoint", 1), ("sum", 0), ("sum", 1), ("sum", 2), ("sum", 3), ("adjoint", 2), ("adjoint", 3),
    ("sum", 4), ("sum", 5), ("out", 2), ("out", 3), ("out", 4), ("out", 0), ("sum", 6), ("sum", 7), ("out", 5),
    ("gate", 2), ("out", 1), ("gate", 3), ("gate", 0), ("out", 6), ("out", 7), ("back", 2), ("back", 3), ("gate", 1),
    ("back", 0), ("gate", 5), ("gate", 4), ("gate", 6), ("gate", 7), ("own", 3), ("back", 1), ("back", 5),
    ("own", 1), ("back", 4), ("pass", 3), ("pass", 2), ("cross", 7), ("back", 6), ("pass", 0), ("own", 5),
    ("pass", 1), ("forward", 3), ("back", 7), ("pass", 5), ("forward", 1), ("pass", 4), ("own", 7), ("pass", 7),
    ("pass", 6), ("forward", 5), ("forward", 7),
]


def schedule(chunks, parts, late):
    steps = chunks * parts
    names = ["sum", "out", "gate", "back", "pass"]
    ops = [("adjoint", ch) for ch in range(chunks)]
    for k in range(steps):
        ops += [(name, k) for name in names]
        if k >= steps - late:
            ops.append(("cross", k))
        if k % parts == parts - 1:
            ops += [("own", k), ("forward", k)]
    if late and len(ops) == len(ORDER):
        assert sorted(ops) == sorted(ORDER)
        return ORDER
    place = lambda op: LAGS[op[0]] + op[1] * (parts if op[0] == "adjoint" else 1)
    return sorted(ops, key=place)


def shards(nf, npanel, wavefield, direct, left_factors, right_factors, tile_src, onset):
    panels, slots = tile_src.shape
    rows, width = right_factors.shape[3:]
    virtual = wavefield.shape[2]
    blocks = SRC_TILES * rows // LANES
    chunks = blocks // npanel
    ny = npanel // 2
    vp = virtual // nf
    pair = 2 * virtual
    parts = halves_of(vp)
    vh = vp // parts
    steps = chunks * parts
    prow = pair // parts
    early, late = (2, 1) if ny == 2 and steps > 2 + 1 else (0, 0)
    left = jnp.transpose(left_factors[0], (1, 0, 2))
    hbm = pl.BlockSpec(memory_space=pl.ANY)
    dma = lambda *n: pltpu.SemaphoreType.DMA(n) if n else pltpu.SemaphoreType.DMA
    split_buf = [pltpu.VMEM((panels, SRC_TILES, rows, width), BF16)] * 2
    if vh % 8 == 0:
        shaped = lambda x: x.reshape(2, nf, parts, vh, x.shape[-1])
        kept = (panels, parts, 2, nf, vh, rows)
    else:
        shaped = lambda x: x
        kept = (panels, 2, virtual, rows)
    field_in, direct_in = shaped(wavefield[0]), shaped(direct[0])
    out = pl.pallas_call(
        functools.partial(marchenko_kernel, nf, ny, chunks, early, late),
        in_specs=[hbm] * 6,
        out_specs=pl.BlockSpec(memory_space=pltpu.VMEM),
        out_shape=pltpu.VMEM(direct_in.shape, F32),
        scratch_shapes=[
            pltpu.SMEM(tile_src.shape, jnp.int32),
            pltpu.VMEM(onset.shape, jnp.int32),
            pltpu.VMEM(kept, F32),
            pltpu.VMEM(kept, F32),
            [pltpu.VMEM((slots, rows, width), F32)] * panels,
            [pltpu.VMEM((slots, rows, width), F32)] * panels,
            pltpu.VMEM((panels, pair, 3 * rows), BF16),
            *split_buf,
            *split_buf,
            pltpu.VMEM((chunks, ny, 2, parts, prow, LANES), F32),
            pltpu.VMEM((steps, ny, prow, LANES), F32),
            pltpu.VMEM((steps, ny, prow, LANES), F32),
            pltpu.VMEM((steps, ny - 1, prow, LANES), F32),
            pltpu.VMEM((steps, 2, nf, vh, LANES), F32),
            pltpu.VMEM((steps, nf, 2, vh, LANES), F32),
            pltpu.VMEM((steps, nf, 2, vh, LANES), F32),
            pltpu.VMEM((blocks, parts, 2, nf, vh, LANES), F32),
            pltpu.VMEM((pair, LANES), F32),
            pltpu.VMEM((max(early, 1), ny, 2, nf, vh, LANES), F32),
            pltpu.VMEM((max(early, 1), ny, nf, 2, vh, LANES), F32),
            pltpu.VMEM((max(early, 1), ny - 1, nf, 2, vh, LANES), F32),
            pltpu.VMEM((ny - 1, nf, 2, vh, LANES), F32),
            dma(), dma(),
            dma(), dma(), dma(panels), dma(panels),
            dma(), dma(steps), dma(), dma(steps + 1), dma(), dma(steps),
            dma(), dma(steps + 1), dma(), dma(steps + 1, ny - 1), dma(), dma(chunks, ny),
            dma(), dma(max(early, 1)), dma(), dma(ny - 1),
        ],
        compiler_params=pltpu.CompilerParams(collective_id=0, has_side_effects=True),
        name="marchenko",
    )(tile_src, onset, field_in, direct_in, left, right_factors[0])
    return out.reshape(direct.shape)


def solution(mesh):
    in_specs = (
        P("freq", None, None, "panel"),
        P("freq", None, None, "panel"),
        P("freq", "panel", None, None),
        P("freq", "panel", None, None, None),
        P("panel", None),
        P("freq", None),
    )
    out_specs = P("freq", None, None, "panel")
    body = functools.partial(shards, mesh.shape["freq"], mesh.shape["panel"])
    return jax.shard_map(body, mesh=mesh, in_specs=in_specs, out_specs=out_specs, check_vma=False)
```

```python
import functools
import math

import jax
import jax.numpy as jnp
from jax import lax
from jax.experimental import pallas as pl
from jax.experimental.pallas import tpu as pltpu
from jax.sharding import PartitionSpec as P

NT = 1024
FIRST_BIN = 8
SRC_TILES = 8
LANES = 128
BF16 = jnp.bfloat16
F32 = jnp.float32
NN = (((1,), (0,)), ((), ()))
NT_DIMS = (((1,), (1,)), ((), ()))


def split(x):
    high = x.astype(BF16)
    return high, (x - high.astype(F32)).astype(BF16)


def mxu(a, b, dims):
    return lax.dot_general(a, b, dims, preferred_element_type=F32)


def lanes(*parts):
    return jnp.concatenate(parts, axis=1)


def pair_coef(products):
    rows, width = products.shape
    first, second = products[: rows // 2], products[rows // 2 :]
    lane = lax.broadcasted_iota(jnp.int32, first.shape, 1)
    sign = jnp.where(lane < width // 2, 1.0, -1.0).astype(F32)
    swap = lambda x: pltpu.roll(x, width // 2, 1)
    return jnp.concatenate([first + sign * swap(second), second - sign * swap(first)], axis=0)

def gate_tables(count):
    assert 2 * (FIRST_BIN + count - 1) < NT
    cot = lambda m: 1.0 / math.tan(math.pi * m / NT)
    minus = [[0.0 if f == g else cot(g - f) for g in range(count)] for f in range(count)]
    plus = [[cot(f + g + 2 * FIRST_BIN) for g in range(count)] for f in range(count)]
    real = [[0.5 * (minus[f][g] + plus[f][g]) for g in range(count)] for f in range(count)]
    imag = [[0.5 * (plus[f][g] - minus[f][g]) for g in range(count)] for f in range(count)]
    return real, imag


def gate_map(xr, xi, tables):
    real, imag = tables
    count = len(xr)
    total = functools.reduce(lambda a, b: a + b, xr)
    gr, gi = [], []
    for f in range(count):
        a = 0.5 * xr[f] - total
        b = 0.5 * xi[f]
        for g in range(count):
            a = a + real[f][g] * xi[g]
            b = b + imag[f][g] * xr[g]
        gr.append(a)
        gi.append(b)
    return gr, gi


def gate(xr, xi, c1, s1, mark, tables):
    count = len(xr)
    scale = 0.5 / math.sqrt(count * NT)
    ec, es = c1, s1
    power = 1
    while power * 2 <= FIRST_BIN:
        ec, es = ec * ec - es * es, 2.0 * ec * es
        power *= 2
    while power < FIRST_BIN:
        ec, es = ec * c1 - es * s1, ec * s1 + es * c1
        power += 1
    cs, sn = [], []
    for f in range(count):
        cs.append(ec)
        sn.append(es)
        ec, es = ec * c1 - es * s1, ec * s1 + es * c1
    yr = [xr[f] * cs[f] - xi[f] * sn[f] for f in range(count)]
    yi = [xr[f] * sn[f] + xi[f] * cs[f] for f in range(count)]
    hr, hi = gate_map(yr, yi, tables)
    gr, gi = gate_map(xr, xi, tables)
    br = [scale * (cs[f] * hr[f] + sn[f] * hi[f] - gr[f] + mark * xr[f]) for f in range(count)]
    bi = [scale * (cs[f] * hi[f] - sn[f] * hr[f] - gi[f] + mark * xi[f]) for f in range(count)]
    return br, bi


def unit(mark):
    quarter = NT // 4
    phase = mark & (NT - 1)
    quad = lax.shift_right_logical(phase + quarter // 2, quarter.bit_length() - 1)
    x = (2.0 * math.pi / NT) * (phase - quad * quarter).astype(F32)
    z = x * x
    c = jnp.full_like(x, 1.0 / math.factorial(10))
    s = jnp.full_like(x, 1.0 / math.factorial(11))
    for n in (8, 6, 4, 2, 0):
        c = 1.0 / math.factorial(n) - z * c
    for n in (9, 7, 5, 3, 1):
        s = 1.0 / math.factorial(n) - z * s
    s = s * x
    quad = quad & 3
    swap = (quad & 1) == 1
    cos = jnp.where(swap, s, c)
    sin = jnp.where(swap, c, s)
    cos = jnp.where((quad == 1) | (quad == 2), -cos, cos)
    sin = jnp.where(quad >= 2, -sin, sin)
    return cos, sin


def halves_of(vp):
    return 2 if vp % 16 == 0 else 1


def marchenko_kernel(
    nf, ny, chunks, early, late, tile_hbm, onset_hbm, field_hbm, direct_hbm, left_hbm, right_hbm, out_ref,
    tile_ref, onset_ref, field, direct, left, right, fcat, left_h, left_l, right_h, right_l,
    part, buf1, sums, buf2, xbuf, rbuf, obuf, source, chosen_ref, xfirst, rfirst, yfirst, ylast,
    tile_sem, onset_sem, field_sem, direct_sem, left_sem, right_sem,
    s1s, s1r, s2s, s2r, s3s, s3r, s4s, s4r, s5s, s5r, s6s, s6r, s7s, s7r, s8s, s8r,
):
    tables = gate_tables(nf)
    panels, (slots, rows, width) = len(right), right[0].shape
    parts, prow = part.shape[3:5]
    pair = parts * prow
    virtual = pair // 2
    vp = virtual // nf
    vh = vp // parts
    aligned = vh % 8 == 0
    blocks = rows // LANES
    np_ = 2 * ny
    tiles = np_ // blocks
    steps = chunks * parts
    me = lax.axis_index("freq")
    q = lax.axis_index("panel")
    y, c = q // 2, q % 2
    partner = {"panel": y * 2 + 1 - c}
    ypeer = [{"panel": ((y + d) % ny) * 2 + c} for d in range(ny)]
    fpeer = [{"freq": (me + d) % nf} for d in range(nf)]
    MESH = pl.DeviceIdType.MESH

    tile_load = pltpu.make_async_copy(tile_hbm, tile_ref, tile_sem)
    onset_load = pltpu.make_async_copy(onset_hbm, onset_ref, onset_sem)
    loads_a, loads_b, loads_c = [], [], []
    for p in range(panels):
        cols = pl.ds(p * rows, rows)
        if aligned:
            group = [
                pltpu.make_async_copy(field_hbm.at[:, :, h, :, cols], field.at[p, h], field_sem)
                for h in range(parts)
            ]
            for h in range(parts):
                loads_c.append(
                    pltpu.make_async_copy(direct_hbm.at[:, :, h, :, cols], direct.at[p, h], direct_sem)
                )
        else:
            group = [pltpu.make_async_copy(field_hbm.at[:, :, cols], field.at[p], field_sem)]
            loads_c.append(pltpu.make_async_copy(direct_hbm.at[:, :, cols], direct.at[p], direct_sem))
        group.append(pltpu.make_async_copy(left_hbm.at[:, cols, :], left[p], left_sem.at[p]))
        loads_a.append(group)
        loads_b.append(pltpu.make_async_copy(right_hbm.at[p], right[p], right_sem.at[p]))
    tile_load.start()
    for group in loads_a:
        for copy in group[:-1]:
            copy.start()
    for group in loads_a:
        group[-1].start()

    barrier = pltpu.get_barrier_semaphore()
    for dev in [partner] + ypeer[1:] + fpeer[1:]:
        pl.semaphore_signal(barrier, inc=1, device_id=dev, device_id_type=MESH)

    def arrived(ref, sem):
        pltpu.make_async_copy(ref, ref, sem).wait()

    def slot_of(p, j):
        slot = jnp.int32(0)
        live = jnp.int32(0)
        for s in range(slots):
            hit = tile_ref[p, s] == j
            slot = jnp.where(hit, jnp.int32(s), slot)
            live = jnp.where(hit, jnp.int32(1), live)
        return slot, live.astype(F32)

    def send(src, dst, ssem, rsem, device):
        copy = pltpu.make_async_remote_copy(
            src_ref=src, dst_ref=dst, send_sem=ssem, recv_sem=rsem, device_id=device, device_id_type=MESH
        )
        copy.start()

    def coef_of(products):
        count = products.shape[0] // prow
        return jnp.concatenate([pair_coef(products[h * prow : (h + 1) * prow]) for h in range(count)], axis=0)

    def block(yy, cc, ch):
        return ch * np_ + yy * 2 + cc

    order = list(range(1, ny)) + [0]
    half = prow // 2
    whole = [(slice(0, 2), 0)]

    def lines(i):
        return slice(0, prow) if isinstance(i, slice) else slice(i * half, (i + 1) * half)

    def entering(k):
        return [(0, 0), (1, steps - k)] if k == early else whole

    def leaving(k):
        return [(i, i) for i in range(2)] if k == steps - 1 and not late else whole


    def stage_adjoint(ch):
        first = ch * tiles
        if ch == 0:
            tile_load.wait()
            for copy in loads_b:
                copy.start()
            arrived(field, field_sem)
            for p in range(panels):
                fh, fl = split(field[p].reshape(pair, rows))
                fcat[p, :, :rows] = fh
                fcat[p, :, rows : 2 * rows] = fh
                fcat[p, :, 2 * rows :] = fl
            for p in range(panels):
                arrived(left[p], left_sem.at[p])
        found = [[slot_of(p, first + t) for t in range(tiles)] for p in range(panels)]
        coefs = [[None] * panels for _ in range(tiles)]
        for p in range(panels):
            for t0 in range(0, tiles, 2):
                sides = []
                for t in range(t0, min(t0 + 2, tiles)):
                    slot, live = found[p][t]
                    h, l = split(left[p][slot] * live)
                    left_h[p, first + t] = h
                    left_l[p, first + t] = l
                    sides.append(jnp.concatenate([h, l, h], axis=0))
                products = mxu(fcat[p], lanes(*sides), NN)
                for i in range(len(sides)):
                    coefs[t0 + i][p] = split(coef_of(products[:, i * width : (i + 1) * width]))
        step = (panels + 1) // 2 if ch == 0 else panels
        sums_t = [None] * tiles
        for p0 in range(0, panels, step):
            for t in range(tiles):
                ins, outs = [], []
                for p in range(p0, min(p0 + step, panels)):
                    if ch == 0 and t == 0:
                        arrived(right[p], right_sem.at[p])
                    rh, rl = split(right[p][found[p][t][0]])
                    right_h[p, first + t] = rh
                    right_l[p, first + t] = rl
                    h, l = coefs[t][p]
                    ins += [h, l, h]
                    outs += [rh, rh, rl]
                more = mxu(lanes(*ins), lanes(*outs), NT_DIMS)
                sums_t[t] = more if p0 == 0 else sums_t[t] + more
        for t, tile in enumerate(sums_t):
            for b in range(blocks):
                for h in range(parts):
                    part[ch, t, b, h] = tile[h * prow : (h + 1) * prow, b * LANES : (b + 1) * LANES]
        if ch == 0:
            for copy in [onset_load] + loads_c:
                copy.start()
            pl.semaphore_wait(barrier, 1 + (ny - 1) + (nf - 1))
        for h in range(parts):
            k = ch * parts + h
            send(part.at[ch, :, 1 - c, h], buf1.at[k], s1s, s1r.at[k], partner)

    def stage_sum(k):
        ch, h = divmod(k, parts)
        arrived(buf1.at[k], s1r.at[k])
        if k < early:
            for d in range(ny):
                yy = (y + d) % ny
                spread(xfirst.at[k, d], part[ch, yy, c, h] + buf1[k, yy], 0)
            for d in range(1, nf):
                to = (me + d) % nf
                send(xfirst.at[k, :, :, to], rfirst.at[k, :, me], s7s, s7r.at[k], fpeer[d])
            rfirst[k, :, me] = xfirst[k, :, :, me]
            return
        for d in order:
            yy = (y + d) % ny
            sums[k, d] = part[ch, yy, c, h] + buf1[k, yy]
            if d:
                for i, at in entering(k):
                    send(sums.at[k, d, lines(i)], buf2.at[k, d - 1, lines(i)], s2s, s2r.at[k + at], ypeer[d])

    def spread(ref, total, first):
        for r in range(total.shape[0] // vh):
            ref[first + r // nf, r % nf] = total[r * vh : (r + 1) * vh]

    def stage_out(k):
        if k < early:
            arrived(rfirst.at[k, :, : nf - 1], s7r.at[k])
            for d in range(1, ny):
                send(rfirst.at[k, d], yfirst.at[k, d - 1], s2s, s2r.at[k], ypeer[d])
            return
        for i, at in entering(k):
            total = sums[k, 0, lines(i)]
            arrived(buf2.at[k, :, lines(i)], s2r.at[k + at])
            for d in range(1, ny):
                total = total + buf2[k, d - 1, lines(i)]
            spread(xbuf.at[k], total, 0 if isinstance(i, slice) else i)
            for d in range(1, nf):
                to = (me + d) % nf
                send(xbuf.at[k, i, to], rbuf.at[k, me, i], s3s, s3r.at[k], fpeer[d])
        rbuf[k, me] = xbuf[k, :, me]

    def stage_gate(k):
        ch, h = divmod(k, parts)
        at = block(y, c, ch)
        if not gates:
            onset_load.wait()
        gates.append(k)
        mark = onset_ref[h * vh : (h + 1) * vh, pl.ds(pl.multiple_of(at * LANES, LANES), LANES)]
        cos, sin = unit(mark)
        if k < early:
            arrived(yfirst.at[k], s2r.at[k])
            both = [[rfirst[k, 0, f, i] for f in range(nf)] for i in range(2)]
            for d in range(1, ny):
                both = [[both[i][f] + yfirst[k, d - 1, f, i] for f in range(nf)] for i in range(2)]
            xr, xi = both
        else:
            arrived(rbuf.at[k, : nf - 1], s3r.at[k])
            xr = [rbuf[k, f, 0] for f in range(nf)]
            xi = [rbuf[k, f, 1] for f in range(nf)]
        br, bi = gate(xr, xi, cos, sin, mark.astype(F32), tables)
        for f in range(nf):
            obuf[k, f, 0] = br[f]
            obuf[k, f, 1] = bi[f]
        for i, sem in leaving(k):
            for d in range(1, nf):
                to = (me + d) % nf
                send(obuf.at[k, to, i], source.at[at, h, i, me], s4s, s4r.at[k + sem], fpeer[d])
        source[at, h, :, me] = obuf[k, me]
        if k >= steps - late:
            for d in range(1, ny):
                send(obuf.at[k], ylast.at[d - 1], s5s, s5r.at[k, d - 1], ypeer[d])

    def stage_cross(k):
        ch, h = divmod(k, parts)
        for d in range(1, ny):
            arrived(ylast.at[d - 1], s5r.at[k, d - 1])
            there = block((y + ny - d) % ny, c, ch)
            for e in range(1, nf):
                to = (me + e) % nf
                send(ylast.at[d - 1, to], source.at[there, h, :, me], s8s, s8r.at[d - 1], fpeer[e])
            source[there, h, :, me] = ylast[d - 1, me]

    def stage_back(k):
        ch, h = divmod(k, parts)
        for i, sem in leaving(k):
            arrived(obuf.at[k, : nf - 1, i], s4r.at[k + sem])
            at = source.at[block(y, c, ch), h, i]
            if k < steps - late:
                for d in range(1, ny):
                    send(at, at, s5s, s5r.at[k + sem, d - 1], ypeer[d])
            send(at, at, s6s, s6r.at[ch, 0], partner)

    def stage_pass(k):
        ch, h = divmod(k, parts)
        for i, sem in leaving(k):
            for d in range(1, ny):
                at = source.at[block((y + ny - d) % ny, c, ch), h, i]
                if k < steps - late:
                    arrived(at, s5r.at[k + sem, d - 1])
                else:
                    arrived(obuf.at[k, : nf - 1], s8r.at[d - 1])
                send(at, at, s6s, s6r.at[ch, d], partner)

    def load_block(b):
        if aligned:
            return source[b].reshape(pair, LANES)
        for i in range(2 * nf):
            chosen_ref[i * vh : (i + 1) * vh, :] = source[b, 0, i // nf, i % nf]
        return chosen_ref[...]

    applied = []
    gates = []

    def apply(items):
        found = []
        for ch, d in items:
            yy = (y + ny - d) % ny
            j = ch * tiles + yy
            arrived(source.at[block(yy, 1 - c, ch)], s6r.at[ch, d])
            h, l = split(lanes(*[load_block(j * blocks + b) for b in range(blocks)]))
            rh = lanes(*[right_h[p, j] for p in range(panels)])
            rl = lanes(*[right_l[p, j] for p in range(panels)])
            found.append((j, mxu(lanes(h, h, l), jnp.concatenate([rh, rl, rh], axis=0), NN)))
        if not applied:
            arrived(direct, direct_sem)
        applied.extend(items)
        last = len(applied) == chunks * ny
        for p in range(panels):
            ins, outs = [], []
            for j, products in found:
                ph, plow = split(coef_of(products[:, p * width : (p + 1) * width]))
                lh, ll = left_h[p, j], left_l[p, j]
                ins += [ph, ph, plow]
                outs += [lh, ll, lh]
            total = mxu(lanes(*ins), lanes(*outs), NT_DIMS)
            done = direct[p] - total.reshape(direct.shape[1:])
            if not last:
                direct[p] = done
            elif aligned:
                for i in range(parts):
                    out_ref[:, :, i, :, p * rows : (p + 1) * rows] = done[i]
            else:
                out_ref[:, :, p * rows : (p + 1) * rows] = done

    def tiles_of(stage, k):
        return [(k // parts, d) for d in (range(1) if stage == "own" else range(1, ny))]

    assert blocks == 2
    run = {"adjoint": stage_adjoint, "sum": stage_sum, "out": stage_out, "gate": stage_gate, "back": stage_back,
           "pass": stage_pass, "cross": stage_cross}
    held = []
    plan = schedule(chunks, parts, late)
    for n, (stage, k) in enumerate(plan):
        if stage in run:
            run[stage](k)
            continue
        held += tiles_of(stage, k)
        more = n + 2 < len(plan) and plan[n + 1][0] not in run
        while held and (len(held) >= GROUP or not more):
            apply(held[:GROUP])
            del held[:GROUP]
    arrived(buf1, s1s)
    arrived(buf2, s2s)
    arrived(rbuf.at[early:, : nf - 1], s3s)
    if early:
        arrived(rfirst.at[:, :, : nf - 1], s7s)
    arrived(obuf.at[:, : nf - 1], s4s)
    arrived(buf2, s5s)
    if late:
        arrived(ylast.at[:, : nf - 1], s8s)
    arrived(buf1, s6s)


LAGS = {
    "adjoint": -8, "sum": -5.5, "out": 0, "gate": 2.5, "cross": 5.2, "back": 5.3, "pass": 6.3, "own": 6.4, "forward": 7.4,
}
GROUP = 2
ORDER = [
    ("adjoint", 0), ("adjoint", 1), ("sum", 0), ("sum", 1), ("sum", 2), ("sum", 3), ("adjoint", 2), ("adjoint", 3),
    ("sum", 4), ("sum", 5), ("out", 2), ("out", 3), ("out", 4), ("out", 0), ("sum", 6), ("sum", 7), ("out", 5),
    ("gate", 2), ("out", 1), ("gate", 3), ("gate", 0), ("out", 6), ("out", 7), ("back", 2), ("gate", 1), ("back", 3),
    ("back", 0), ("gate", 5), ("gate", 4), ("gate", 6), ("gate", 7), ("own", 3), ("back", 1), ("back", 5),
    ("own", 1), ("back", 4), ("pass", 3), ("pass", 2), ("cross", 7), ("back", 6), ("pass", 0), ("own", 5),
    ("pass", 1), ("forward", 3), ("back", 7), ("pass", 5), ("forward", 1), ("pass", 4), ("own", 7), ("pass", 7),
    ("pass", 6), ("forward", 5), ("forward", 7),
]


def schedule(chunks, parts, late):
    steps = chunks * parts
    names = ["sum", "out", "gate", "back", "pass"]
    ops = [("adjoint", ch) for ch in range(chunks)]
    for k in range(steps):
        ops += [(name, k) for name in names]
        if k >= steps - late:
            ops.append(("cross", k))
        if k % parts == parts - 1:
            ops += [("own", k), ("forward", k)]
    if late and len(ops) == len(ORDER):
        assert sorted(ops) == sorted(ORDER)
        return ORDER
    place = lambda op: LAGS[op[0]] + op[1] * (parts if op[0] == "adjoint" else 1)
    return sorted(ops, key=place)


def shards(nf, npanel, wavefield, direct, left_factors, right_factors, tile_src, onset):
    panels, slots = tile_src.shape
    rows, width = right_factors.shape[3:]
    virtual = wavefield.shape[2]
    blocks = SRC_TILES * rows // LANES
    chunks = blocks // npanel
    ny = npanel // 2
    vp = virtual // nf
    pair = 2 * virtual
    parts = halves_of(vp)
    vh = vp // parts
    steps = chunks * parts
    prow = pair // parts
    early, late = (2, 1) if ny == 2 and steps > 2 + 1 else (0, 0)
    left = jnp.transpose(left_factors[0], (1, 0, 2))
    hbm = pl.BlockSpec(memory_space=pl.ANY)
    dma = lambda *n: pltpu.SemaphoreType.DMA(n) if n else pltpu.SemaphoreType.DMA
    split_buf = [pltpu.VMEM((panels, SRC_TILES, rows, width), BF16)] * 2
    if vh % 8 == 0:
        shaped = lambda x: x.reshape(2, nf, parts, vh, x.shape[-1])
        kept = (panels, parts, 2, nf, vh, rows)
    else:
        shaped = lambda x: x
        kept = (panels, 2, virtual, rows)
    field_in, direct_in = shaped(wavefield[0]), shaped(direct[0])
    out = pl.pallas_call(
        functools.partial(marchenko_kernel, nf, ny, chunks, early, late),
        in_specs=[hbm] * 6,
        out_specs=pl.BlockSpec(memory_space=pltpu.VMEM),
        out_shape=pltpu.VMEM(direct_in.shape, F32),
        scratch_shapes=[
            pltpu.SMEM(tile_src.shape, jnp.int32),
            pltpu.VMEM(onset.shape, jnp.int32),
            pltpu.VMEM(kept, F32),
            pltpu.VMEM(kept, F32),
            [pltpu.VMEM((slots, rows, width), F32)] * panels,
            [pltpu.VMEM((slots, rows, width), F32)] * panels,
            pltpu.VMEM((panels, pair, 3 * rows), BF16),
            *split_buf,
            *split_buf,
            pltpu.VMEM((chunks, ny, 2, parts, prow, LANES), F32),
            pltpu.VMEM((steps, ny, prow, LANES), F32),
            pltpu.VMEM((steps, ny, prow, LANES), F32),
            pltpu.VMEM((steps, ny - 1, prow, LANES), F32),
            pltpu.VMEM((steps, 2, nf, vh, LANES), F32),
            pltpu.VMEM((steps, nf, 2, vh, LANES), F32),
            pltpu.VMEM((steps, nf, 2, vh, LANES), F32),
            pltpu.VMEM((blocks, parts, 2, nf, vh, LANES), F32),
            pltpu.VMEM((pair, LANES), F32),
            pltpu.VMEM((max(early, 1), ny, 2, nf, vh, LANES), F32),
            pltpu.VMEM((max(early, 1), ny, nf, 2, vh, LANES), F32),
            pltpu.VMEM((max(early, 1), ny - 1, nf, 2, vh, LANES), F32),
            pltpu.VMEM((ny - 1, nf, 2, vh, LANES), F32),
            dma(), dma(),
            dma(), dma(), dma(panels), dma(panels),
            dma(), dma(steps), dma(), dma(steps + 1), dma(), dma(steps),
            dma(), dma(steps + 1), dma(), dma(steps + 1, ny - 1), dma(), dma(chunks, ny),
            dma(), dma(max(early, 1)), dma(), dma(ny - 1),
        ],
        compiler_params=pltpu.CompilerParams(collective_id=0, has_side_effects=True),
        name="marchenko",
    )(tile_src, onset, field_in, direct_in, left, right_factors[0])
    return out.reshape(direct.shape)


def solution(mesh):
    in_specs = (
        P("freq", None, None, "panel"),
        P("freq", None, None, "panel"),
        P("freq", "panel", None, None),
        P("freq", "panel", None, None, None),
        P("panel", None),
        P("freq", None),
    )
    out_specs = P("freq", None, None, "panel")
    body = functools.partial(shards, mesh.shape["freq"], mesh.shape["panel"])
    return jax.shard_map(body, mesh=mesh, in_specs=in_specs, out_specs=out_specs, check_vma=False)
```

```python
import functools
import math

import jax
import jax.numpy as jnp
from jax import lax
from jax.experimental import pallas as pl
from jax.experimental.pallas import tpu as pltpu
from jax.sharding import PartitionSpec as P

NT = 1024
FIRST_BIN = 8
SRC_TILES = 8
LANES = 128
BF16 = jnp.bfloat16
F32 = jnp.float32
NN = (((1,), (0,)), ((), ()))
NT_DIMS = (((1,), (1,)), ((), ()))


def split(x):
    high = x.astype(BF16)
    return high, (x - high.astype(F32)).astype(BF16)


def mxu(a, b, dims):
    return lax.dot_general(a, b, dims, preferred_element_type=F32)


def lanes(*parts):
    return jnp.concatenate(parts, axis=1)


def pair_coef(products):
    rows, width = products.shape
    first, second = products[: rows // 2], products[rows // 2 :]
    lane = lax.broadcasted_iota(jnp.int32, first.shape, 1)
    sign = jnp.where(lane < width // 2, 1.0, -1.0).astype(F32)
    swap = lambda x: pltpu.roll(x, width // 2, 1)
    return jnp.concatenate([first + sign * swap(second), second - sign * swap(first)], axis=0)

def gate_tables(count):
    assert 2 * (FIRST_BIN + count - 1) < NT
    cot = lambda m: 1.0 / math.tan(math.pi * m / NT)
    minus = [[0.0 if f == g else cot(g - f) for g in range(count)] for f in range(count)]
    plus = [[cot(f + g + 2 * FIRST_BIN) for g in range(count)] for f in range(count)]
    real = [[0.5 * (minus[f][g] + plus[f][g]) for g in range(count)] for f in range(count)]
    imag = [[0.5 * (plus[f][g] - minus[f][g]) for g in range(count)] for f in range(count)]
    return real, imag


def gate_map(xr, xi, tables):
    real, imag = tables
    count = len(xr)
    total = functools.reduce(lambda a, b: a + b, xr)
    gr, gi = [], []
    for f in range(count):
        a = 0.5 * xr[f] - total
        b = 0.5 * xi[f]
        for g in range(count):
            a = a + real[f][g] * xi[g]
            b = b + imag[f][g] * xr[g]
        gr.append(a)
        gi.append(b)
    return gr, gi


def gate(xr, xi, c1, s1, mark, tables):
    count = len(xr)
    scale = 0.5 / math.sqrt(count * NT)
    ec, es = c1, s1
    power = 1
    while power * 2 <= FIRST_BIN:
        ec, es = ec * ec - es * es, 2.0 * ec * es
        power *= 2
    while power < FIRST_BIN:
        ec, es = ec * c1 - es * s1, ec * s1 + es * c1
        power += 1
    cs, sn = [], []
    for f in range(count):
        cs.append(ec)
        sn.append(es)
        ec, es = ec * c1 - es * s1, ec * s1 + es * c1
    yr = [xr[f] * cs[f] - xi[f] * sn[f] for f in range(count)]
    yi = [xr[f] * sn[f] + xi[f] * cs[f] for f in range(count)]
    hr, hi = gate_map(yr, yi, tables)
    gr, gi = gate_map(xr, xi, tables)
    br = [scale * (cs[f] * hr[f] + sn[f] * hi[f] - gr[f] + mark * xr[f]) for f in range(count)]
    bi = [scale * (cs[f] * hi[f] - sn[f] * hr[f] - gi[f] + mark * xi[f]) for f in range(count)]
    return br, bi


def unit(mark):
    quarter = NT // 4
    phase = mark & (NT - 1)
    quad = lax.shift_right_logical(phase + quarter // 2, quarter.bit_length() - 1)
    x = (2.0 * math.pi / NT) * (phase - quad * quarter).astype(F32)
    z = x * x
    c = jnp.full_like(x, 1.0 / math.factorial(10))
    s = jnp.full_like(x, 1.0 / math.factorial(11))
    for n in (8, 6, 4, 2, 0):
        c = 1.0 / math.factorial(n) - z * c
    for n in (9, 7, 5, 3, 1):
        s = 1.0 / math.factorial(n) - z * s
    s = s * x
    quad = quad & 3
    swap = (quad & 1) == 1
    cos = jnp.where(swap, s, c)
    sin = jnp.where(swap, c, s)
    cos = jnp.where((quad == 1) | (quad == 2), -cos, cos)
    sin = jnp.where(quad >= 2, -sin, sin)
    return cos, sin


def halves_of(vp):
    return 2 if vp % 16 == 0 else 1


def marchenko_kernel(
    nf, ny, chunks, early, late, tile_hbm, onset_hbm, field_hbm, direct_hbm, left_hbm, right_hbm, out_ref,
    tile_ref, onset_ref, field, direct, left, right, fcat, left_h, left_l, right_h, right_l,
    part, buf1, sums, buf2, xbuf, rbuf, obuf, source, chosen_ref, xfirst, rfirst, yfirst, ylast,
    tile_sem, onset_sem, field_sem, direct_sem, left_sem, right_sem,
    s1s, s1r, s2s, s2r, s3s, s3r, s4s, s4r, s5s, s5r, s6s, s6r, s7s, s7r, s8s, s8r,
):
    tables = gate_tables(nf)
    panels, (slots, rows, width) = len(right), right[0].shape
    parts, prow = part.shape[3:5]
    pair = parts * prow
    virtual = pair // 2
    vp = virtual // nf
    vh = vp // parts
    aligned = vh % 8 == 0
    blocks = rows // LANES
    np_ = 2 * ny
    tiles = np_ // blocks
    steps = chunks * parts
    me = lax.axis_index("freq")
    q = lax.axis_index("panel")
    y, c = q // 2, q % 2
    partner = {"panel": y * 2 + 1 - c}
    ypeer = [{"panel": ((y + d) % ny) * 2 + c} for d in range(ny)]
    fpeer = [{"freq": (me + d) % nf} for d in range(nf)]
    MESH = pl.DeviceIdType.MESH

    tile_load = pltpu.make_async_copy(tile_hbm, tile_ref, tile_sem)
    onset_load = pltpu.make_async_copy(onset_hbm, onset_ref, onset_sem)
    loads_a, loads_b, loads_c = [], [], []
    for p in range(panels):
        cols = pl.ds(p * rows, rows)
        if aligned:
            group = [
                pltpu.make_async_copy(field_hbm.at[:, :, h, :, cols], field.at[p, h], field_sem)
                for h in range(parts)
            ]
            for h in range(parts):
                loads_c.append(
                    pltpu.make_async_copy(direct_hbm.at[:, :, h, :, cols], direct.at[p, h], direct_sem)
                )
        else:
            group = [pltpu.make_async_copy(field_hbm.at[:, :, cols], field.at[p], field_sem)]
            loads_c.append(pltpu.make_async_copy(direct_hbm.at[:, :, cols], direct.at[p], direct_sem))
        group.append(pltpu.make_async_copy(left_hbm.at[:, cols, :], left[p], left_sem.at[p]))
        loads_a.append(group)
        loads_b.append(pltpu.make_async_copy(right_hbm.at[p], right[p], right_sem.at[p]))
    tile_load.start()
    for group in loads_a:
        for copy in group[:-1]:
            copy.start()
    for group in loads_a:
        group[-1].start()

    barrier = pltpu.get_barrier_semaphore()
    for dev in [partner] + ypeer[1:] + fpeer[1:]:
        pl.semaphore_signal(barrier, inc=1, device_id=dev, device_id_type=MESH)

    def arrived(ref, sem):
        pltpu.make_async_copy(ref, ref, sem).wait()

    def slot_of(p, j):
        slot = jnp.int32(0)
        live = jnp.int32(0)
        for s in range(slots):
            hit = tile_ref[p, s] == j
            slot = jnp.where(hit, jnp.int32(s), slot)
            live = jnp.where(hit, jnp.int32(1), live)
        return slot, live.astype(F32)

    def send(src, dst, ssem, rsem, device):
        copy = pltpu.make_async_remote_copy(
            src_ref=src, dst_ref=dst, send_sem=ssem, recv_sem=rsem, device_id=device, device_id_type=MESH
        )
        copy.start()

    def coef_of(products):
        count = products.shape[0] // prow
        return jnp.concatenate([pair_coef(products[h * prow : (h + 1) * prow]) for h in range(count)], axis=0)

    def block(yy, cc, ch):
        return ch * np_ + yy * 2 + cc

    order = list(range(1, ny)) + [0]
    half = prow // 2
    whole = [(slice(0, 2), 0)]

    def lines(i):
        return slice(0, prow) if isinstance(i, slice) else slice(i * half, (i + 1) * half)

    def entering(k):
        return [(0, 0), (1, steps - k)] if k == early else whole

    def leaving(k):
        return [(i, i) for i in range(2)] if k == steps - 1 and not late else whole


    def stage_adjoint(ch):
        first = ch * tiles
        if ch == 0:
            tile_load.wait()
            for copy in loads_b:
                copy.start()
            arrived(field, field_sem)
            for p in range(panels):
                fh, fl = split(field[p].reshape(pair, rows))
                fcat[p, :, :rows] = fh
                fcat[p, :, rows : 2 * rows] = fh
                fcat[p, :, 2 * rows :] = fl
            for p in range(panels):
                arrived(left[p], left_sem.at[p])
        found = [[slot_of(p, first + t) for t in range(tiles)] for p in range(panels)]
        coefs = [[None] * panels for _ in range(tiles)]
        for p in range(panels):
            for t0 in range(0, tiles, 2):
                sides = []
                for t in range(t0, min(t0 + 2, tiles)):
                    slot, live = found[p][t]
                    h, l = split(left[p][slot] * live)
                    left_h[p, first + t] = h
                    left_l[p, first + t] = l
                    sides.append(jnp.concatenate([h, l, h], axis=0))
                products = mxu(fcat[p], lanes(*sides), NN)
                for i in range(len(sides)):
                    coefs[t0 + i][p] = split(coef_of(products[:, i * width : (i + 1) * width]))
        step = (panels + 1) // 2 if ch == 0 else panels
        sums_t = [None] * tiles
        for p0 in range(0, panels, step):
            for t in range(tiles):
                ins, outs = [], []
                for p in range(p0, min(p0 + step, panels)):
                    if ch == 0 and t == 0:
                        arrived(right[p], right_sem.at[p])
                    rh, rl = split(right[p][found[p][t][0]])
                    right_h[p, first + t] = rh
                    right_l[p, first + t] = rl
                    h, l = coefs[t][p]
                    ins += [h, l, h]
                    outs += [rh, rh, rl]
                more = mxu(lanes(*ins), lanes(*outs), NT_DIMS)
                sums_t[t] = more if p0 == 0 else sums_t[t] + more
        for t, tile in enumerate(sums_t):
            for b in range(blocks):
                for h in range(parts):
                    part[ch, t, b, h] = tile[h * prow : (h + 1) * prow, b * LANES : (b + 1) * LANES]
        if ch == 0:
            for copy in [onset_load] + loads_c:
                copy.start()
            pl.semaphore_wait(barrier, 1 + (ny - 1) + (nf - 1))
        for h in range(parts):
            k = ch * parts + h
            send(part.at[ch, :, 1 - c, h], buf1.at[k], s1s, s1r.at[k], partner)

    def stage_sum(k):
        ch, h = divmod(k, parts)
        arrived(buf1.at[k], s1r.at[k])
        if k < early:
            for d in range(ny):
                yy = (y + d) % ny
                spread(xfirst.at[k, d], part[ch, yy, c, h] + buf1[k, yy], 0)
            for d in range(1, nf):
                to = (me + d) % nf
                send(xfirst.at[k, :, :, to], rfirst.at[k, :, me], s7s, s7r.at[k], fpeer[d])
            rfirst[k, :, me] = xfirst[k, :, :, me]
            return
        for d in order:
            yy = (y + d) % ny
            sums[k, d] = part[ch, yy, c, h] + buf1[k, yy]
            if d:
                for i, at in entering(k):
                    send(sums.at[k, d, lines(i)], buf2.at[k, d - 1, lines(i)], s2s, s2r.at[k + at], ypeer[d])

    def spread(ref, total, first):
        for r in range(total.shape[0] // vh):
            ref[first + r // nf, r % nf] = total[r * vh : (r + 1) * vh]

    def stage_out(k):
        if k < early:
            arrived(rfirst.at[k, :, : nf - 1], s7r.at[k])
            for d in range(1, ny):
                send(rfirst.at[k, d], yfirst.at[k, d - 1], s2s, s2r.at[k], ypeer[d])
            return
        for i, at in entering(k):
            total = sums[k, 0, lines(i)]
            arrived(buf2.at[k, :, lines(i)], s2r.at[k + at])
            for d in range(1, ny):
                total = total + buf2[k, d - 1, lines(i)]
            spread(xbuf.at[k], total, 0 if isinstance(i, slice) else i)
            for d in range(1, nf):
                to = (me + d) % nf
                send(xbuf.at[k, i, to], rbuf.at[k, me, i], s3s, s3r.at[k], fpeer[d])
        rbuf[k, me] = xbuf[k, :, me]

    def stage_gate(k):
        ch, h = divmod(k, parts)
        at = block(y, c, ch)
        if not gates:
            onset_load.wait()
        gates.append(k)
        mark = onset_ref[h * vh : (h + 1) * vh, pl.ds(pl.multiple_of(at * LANES, LANES), LANES)]
        cos, sin = unit(mark)
        if k < early:
            arrived(yfirst.at[k], s2r.at[k])
            both = [[rfirst[k, 0, f, i] for f in range(nf)] for i in range(2)]
            for d in range(1, ny):
                both = [[both[i][f] + yfirst[k, d - 1, f, i] for f in range(nf)] for i in range(2)]
            xr, xi = both
        else:
            arrived(rbuf.at[k, : nf - 1], s3r.at[k])
            xr = [rbuf[k, f, 0] for f in range(nf)]
            xi = [rbuf[k, f, 1] for f in range(nf)]
        br, bi = gate(xr, xi, cos, sin, mark.astype(F32), tables)
        for f in range(nf):
            obuf[k, f, 0] = br[f]
            obuf[k, f, 1] = bi[f]
        if k >= steps - late:
            for d in range(1, ny):
                send(obuf.at[k], ylast.at[d - 1], s5s, s5r.at[k, d - 1], ypeer[d])
        for i, sem in leaving(k):
            for d in range(1, nf):
                to = (me + d) % nf
                send(obuf.at[k, to, i], source.at[at, h, i, me], s4s, s4r.at[k + sem], fpeer[d])
        source[at, h, :, me] = obuf[k, me]

    def stage_cross(k):
        ch, h = divmod(k, parts)
        for d in range(1, ny):
            arrived(ylast.at[d - 1], s5r.at[k, d - 1])
            there = block((y + ny - d) % ny, c, ch)
            for e in range(1, nf):
                to = (me + e) % nf
                send(ylast.at[d - 1, to], source.at[there, h, :, me], s8s, s8r.at[d - 1], fpeer[e])
            source[there, h, :, me] = ylast[d - 1, me]

    def stage_back(k):
        ch, h = divmod(k, parts)
        for i, sem in leaving(k):
            arrived(obuf.at[k, : nf - 1, i], s4r.at[k + sem])
            at = source.at[block(y, c, ch), h, i]
            if k < steps - late:
                for d in range(1, ny):
                    send(at, at, s5s, s5r.at[k + sem, d - 1], ypeer[d])
            send(at, at, s6s, s6r.at[ch, 0], partner)

    def stage_pass(k):
        ch, h = divmod(k, parts)
        for i, sem in leaving(k):
            for d in range(1, ny):
                at = source.at[block((y + ny - d) % ny, c, ch), h, i]
                if k < steps - late:
                    arrived(at, s5r.at[k + sem, d - 1])
                else:
                    arrived(obuf.at[k, : nf - 1], s8r.at[d - 1])
                send(at, at, s6s, s6r.at[ch, d], partner)

    def load_block(b):
        if aligned:
            return source[b].reshape(pair, LANES)
        for i in range(2 * nf):
            chosen_ref[i * vh : (i + 1) * vh, :] = source[b, 0, i // nf, i % nf]
        return chosen_ref[...]

    applied = []
    gates = []

    def apply(items):
        found = []
        for ch, d in items:
            yy = (y + ny - d) % ny
            j = ch * tiles + yy
            arrived(source.at[block(yy, 1 - c, ch)], s6r.at[ch, d])
            h, l = split(lanes(*[load_block(j * blocks + b) for b in range(blocks)]))
            rh = lanes(*[right_h[p, j] for p in range(panels)])
            rl = lanes(*[right_l[p, j] for p in range(panels)])
            found.append((j, mxu(lanes(h, h, l), jnp.concatenate([rh, rl, rh], axis=0), NN)))
        if not applied:
            arrived(direct, direct_sem)
        applied.extend(items)
        last = len(applied) == chunks * ny
        for p in range(panels):
            ins, outs = [], []
            for j, products in found:
                ph, plow = split(coef_of(products[:, p * width : (p + 1) * width]))
                lh, ll = left_h[p, j], left_l[p, j]
                ins += [ph, ph, plow]
                outs += [lh, ll, lh]
            total = mxu(lanes(*ins), lanes(*outs), NT_DIMS)
            done = direct[p] - total.reshape(direct.shape[1:])
            if not last:
                direct[p] = done
            elif aligned:
                for i in range(parts):
                    out_ref[:, :, i, :, p * rows : (p + 1) * rows] = done[i]
            else:
                out_ref[:, :, p * rows : (p + 1) * rows] = done

    def tiles_of(stage, k):
        return [(k // parts, d) for d in (range(1) if stage == "own" else range(1, ny))]

    assert blocks == 2
    run = {"adjoint": stage_adjoint, "sum": stage_sum, "out": stage_out, "gate": stage_gate, "back": stage_back,
           "pass": stage_pass, "cross": stage_cross}
    held = []
    plan = schedule(chunks, parts, late)
    for n, (stage, k) in enumerate(plan):
        if stage in run:
            run[stage](k)
            continue
        held += tiles_of(stage, k)
        more = n + 2 < len(plan) and plan[n + 1][0] not in run
        while held and (len(held) >= GROUP or not more):
            apply(held[:GROUP])
            del held[:GROUP]
    arrived(buf1, s1s)
    arrived(buf2, s2s)
    arrived(rbuf.at[early:, : nf - 1], s3s)
    if early:
        arrived(rfirst.at[:, :, : nf - 1], s7s)
    arrived(obuf.at[:, : nf - 1], s4s)
    arrived(buf2, s5s)
    if late:
        arrived(ylast.at[:, : nf - 1], s8s)
    arrived(buf1, s6s)


LAGS = {
    "adjoint": -8, "sum": -5.5, "out": 0, "gate": 2.5, "cross": 5.2, "back": 5.3, "pass": 6.3, "own": 6.4, "forward": 7.4,
}
GROUP = 2
ORDER = [
    ("adjoint", 0), ("adjoint", 1), ("sum", 0), ("sum", 1), ("sum", 2), ("sum", 3), ("adjoint", 2), ("adjoint", 3),
    ("sum", 4), ("sum", 5), ("out", 2), ("out", 3), ("out", 4), ("out", 0), ("sum", 6), ("sum", 7), ("out", 5),
    ("gate", 2), ("out", 1), ("gate", 3), ("gate", 0), ("out", 6), ("out", 7), ("back", 2), ("gate", 1), ("back", 3),
    ("back", 0), ("gate", 5), ("gate", 4), ("gate", 6), ("gate", 7), ("own", 3), ("back", 1), ("back", 5),
    ("own", 1), ("back", 4), ("pass", 3), ("pass", 2), ("cross", 7), ("back", 6), ("pass", 0), ("own", 5),
    ("pass", 1), ("forward", 3), ("back", 7), ("pass", 5), ("forward", 1), ("pass", 4), ("own", 7), ("pass", 7),
    ("pass", 6), ("forward", 5), ("forward", 7),
]


def schedule(chunks, parts, late):
    steps = chunks * parts
    names = ["sum", "out", "gate", "back", "pass"]
    ops = [("adjoint", ch) for ch in range(chunks)]
    for k in range(steps):
        ops += [(name, k) for name in names]
        if k >= steps - late:
            ops.append(("cross", k))
        if k % parts == parts - 1:
            ops += [("own", k), ("forward", k)]
    if late and len(ops) == len(ORDER):
        assert sorted(ops) == sorted(ORDER)
        return ORDER
    place = lambda op: LAGS[op[0]] + op[1] * (parts if op[0] == "adjoint" else 1)
    return sorted(ops, key=place)


def shards(nf, npanel, wavefield, direct, left_factors, right_factors, tile_src, onset):
    panels, slots = tile_src.shape
    rows, width = right_factors.shape[3:]
    virtual = wavefield.shape[2]
    blocks = SRC_TILES * rows // LANES
    chunks = blocks // npanel
    ny = npanel // 2
    vp = virtual // nf
    pair = 2 * virtual
    parts = halves_of(vp)
    vh = vp // parts
    steps = chunks * parts
    prow = pair // parts
    early, late = (2, 1) if ny == 2 and steps > 2 + 1 else (0, 0)
    left = jnp.transpose(left_factors[0], (1, 0, 2))
    hbm = pl.BlockSpec(memory_space=pl.ANY)
    dma = lambda *n: pltpu.SemaphoreType.DMA(n) if n else pltpu.SemaphoreType.DMA
    split_buf = [pltpu.VMEM((panels, SRC_TILES, rows, width), BF16)] * 2
    if vh % 8 == 0:
        shaped = lambda x: x.reshape(2, nf, parts, vh, x.shape[-1])
        kept = (panels, parts, 2, nf, vh, rows)
    else:
        shaped = lambda x: x
        kept = (panels, 2, virtual, rows)
    field_in, direct_in = shaped(wavefield[0]), shaped(direct[0])
    out = pl.pallas_call(
        functools.partial(marchenko_kernel, nf, ny, chunks, early, late),
        in_specs=[hbm] * 6,
        out_specs=pl.BlockSpec(memory_space=pltpu.VMEM),
        out_shape=pltpu.VMEM(direct_in.shape, F32),
        scratch_shapes=[
            pltpu.SMEM(tile_src.shape, jnp.int32),
            pltpu.VMEM(onset.shape, jnp.int32),
            pltpu.VMEM(kept, F32),
            pltpu.VMEM(kept, F32),
            [pltpu.VMEM((slots, rows, width), F32)] * panels,
            [pltpu.VMEM((slots, rows, width), F32)] * panels,
            pltpu.VMEM((panels, pair, 3 * rows), BF16),
            *split_buf,
            *split_buf,
            pltpu.VMEM((chunks, ny, 2, parts, prow, LANES), F32),
            pltpu.VMEM((steps, ny, prow, LANES), F32),
            pltpu.VMEM((steps, ny, prow, LANES), F32),
            pltpu.VMEM((steps, ny - 1, prow, LANES), F32),
            pltpu.VMEM((steps, 2, nf, vh, LANES), F32),
            pltpu.VMEM((steps, nf, 2, vh, LANES), F32),
            pltpu.VMEM((steps, nf, 2, vh, LANES), F32),
            pltpu.VMEM((blocks, parts, 2, nf, vh, LANES), F32),
            pltpu.VMEM((pair, LANES), F32),
            pltpu.VMEM((max(early, 1), ny, 2, nf, vh, LANES), F32),
            pltpu.VMEM((max(early, 1), ny, nf, 2, vh, LANES), F32),
            pltpu.VMEM((max(early, 1), ny - 1, nf, 2, vh, LANES), F32),
            pltpu.VMEM((ny - 1, nf, 2, vh, LANES), F32),
            dma(), dma(),
            dma(), dma(), dma(panels), dma(panels),
            dma(), dma(steps), dma(), dma(steps + 1), dma(), dma(steps),
            dma(), dma(steps + 1 - late), dma(), dma(steps + 1 - late, ny - 1), dma(), dma(chunks, ny),
            dma(), dma(max(early, 1)), dma(), dma(ny - 1),
        ],
        compiler_params=pltpu.CompilerParams(collective_id=0, has_side_effects=True),
        name="marchenko",
    )(tile_src, onset, field_in, direct_in, left, right_factors[0])
    return out.reshape(direct.shape)


def solution(mesh):
    in_specs = (
        P("freq", None, None, "panel"),
        P("freq", None, None, "panel"),
        P("freq", "panel", None, None),
        P("freq", "panel", None, None, None),
        P("panel", None),
        P("freq", None),
    )
    out_specs = P("freq", None, None, "panel")
    body = functools.partial(shards, mesh.shape["freq"], mesh.shape["panel"])
    return jax.shard_map(body, mesh=mesh, in_specs=in_specs, out_specs=out_specs, check_vma=False)
```
